256 devices in a mesh: dp: 8 (over x, y_lo), seq: 32 (over z, y_hi, core).
Axes of the slice: x: 4, y: 4 (y_hi: 2, y_lo: 2; y = y_hi * 2 + y_lo), z: 8, core: 2. Of those that a mesh axis runs over, the one named last changes fastest.
Arguments:
- x_fwd: bfloat16 [131072, 1024], P(('dp', 'seq')), parts along dimension 0, may hold values from -6 to 6
- x_rev: bfloat16 [131072, 1024], P(('dp', 'seq')), parts along dimension 0, may hold values from -6 to 6
- gain: bfloat16 [1024], replicated, may hold values from 0.099609375 to 1.8984375
- w_qkv: bfloat16 [1024, 3072], replicated
Outputs:
- y_fwd: bfloat16 [131072, 1024], P(('dp', 'seq')), parts along dimension 0
- y_rev: bfloat16 [131072, 1024], P(('dp', 'seq')), parts along dimension 0
The draws below stay inside these ranges and needn't reach their ends.
There are 8 independent parts, one for each index of `dp`. The reference program is written for one: setup_inputs(seed, part) draws one part's arguments, and reference() takes and returns one part's arrays. A program takes and returns all parts, laid end to end along the dimension named above; an argument that names none is the same for every part. Nothing has to cross between parts.
All inputs are finite; a program needn't handle non-finite values.
Results may differ from the reference program's by a relative error of at most 0.012.
Values may be sent and summed in bfloat16 or wider, within the bound.
No kernel may reach another device: no remote copies, remote signals or barrier semaphores. Data moves between devices by JAX's collectives and lax.ppermute only.
A program may use at most 128 MiB of HBM per device.

```python
import jax
import jax.numpy as jnp
from jax import lax

D = 1024
HEADS = 16
HEAD_DIM = 64
WINDOW = 512
ROWS = 512
LENGTH = 16384
N_SEQ = 32


def draw_w_qkv(key, part):
    inner = jax.random.fold_in(key, 11)
    first, second, third = jax.random.split(inner, 3)
    base_q = jax.random.normal(first, (D, D), jnp.float32)
    base_k = jax.random.normal(second, (D, D), jnp.float32)
    base_v = jax.random.normal(third, (D, D), jnp.float32)
    query = base_q * (1.4 * D ** (-0.5))
    keys = base_k * (1.4 * D ** (-0.5))
    values = base_v * (3.0 * D ** (-0.5))
    return jnp.concatenate([query, keys, values], axis=1).astype(jnp.bfloat16)


def block_levels(own_key, dims, pieces, least, top_value):
    def one(dim, parts):
        steps = jax.random.uniform(jax.random.fold_in(jax.random.fold_in(own_key, 6), dim), (parts,), jnp.float32, least / len(pieces), top_value / len(pieces))
        return jnp.repeat(jnp.exp(steps), dims[dim] // parts).reshape((-1,) + (1,) * (len(dims) - dim - 1))

    level = one(*pieces[0])
    for cut in pieces[1:]:
        level = level * one(*cut)
    return level


def centred(stream_key, extent, spread, bound, cuts=(), held_as=jnp.bfloat16):
    factor_of = block_levels(stream_key, extent, cuts, -0.22, 0.18) if cuts else 1.0
    drawn = jax.random.normal(stream_key, extent, jnp.float32) * spread * factor_of
    return jnp.minimum(jnp.maximum(drawn, -bound), bound).astype(held_as)


def setup_inputs(seed: int = 0, part: int = 0) -> dict:
    key_list = jax.random.split(jax.random.key(seed), 5)
    own_keys = jax.random.split(jax.random.fold_in(key_list[4], part), 5)
    return {
        "x_fwd": centred(own_keys[0], (LENGTH, D), 1.0, 6.0, ((0, 32),)),
        "x_rev": centred(own_keys[1], (LENGTH, D), 1.0, 6.0, ((0, 32),)),
        "gain": jnp.clip(1.0 + 0.18 * jax.random.normal(key_list[2], (D,), jnp.float32), 0.099609375, 1.8984375).astype(jnp.bfloat16),
        "w_qkv": draw_w_qkv(jax.random.fold_in(key_list[4], 71), part),
    }


def strand_attention(x, gain, w_qkv):
    xf = x.astype(jnp.float32)
    meansq = lax.optimization_barrier(jnp.mean(xf * xf, axis=-1, keepdims=True))
    normed = (xf * lax.rsqrt(meansq + 1e-06) * gain.astype(jnp.float32)).astype(jnp.bfloat16)
    qkv = jnp.dot(normed, w_qkv, preferred_element_type=jnp.float32).astype(jnp.bfloat16)
    query = qkv[:, :D]
    zeros = jnp.zeros((WINDOW, D), jnp.bfloat16)
    keys = jnp.concatenate([zeros, qkv[:, D:2 * D], zeros], axis=0)
    values = jnp.concatenate([zeros, qkv[:, 2 * D:], zeros], axis=0)
    scale = HEAD_DIM ** (-0.5)
    span = ROWS + 2 * WINDOW

    def block(index):
        start = (index * ROWS).astype(jnp.int32)
        qblock = lax.dynamic_slice_in_dim(query, start, ROWS, 0).astype(jnp.float32).reshape(ROWS, HEADS, HEAD_DIM)
        kblock = lax.dynamic_slice_in_dim(keys, start, span, 0).astype(jnp.float32).reshape(span, HEADS, HEAD_DIM)
        vblock = lax.dynamic_slice_in_dim(values, start, span, 0).astype(jnp.float32).reshape(span, HEADS, HEAD_DIM)
        scores = jnp.einsum('rhd,khd->hrk', qblock, kblock) * scale
        qpos = start + jnp.arange(ROWS, dtype=jnp.int32)
        kpos = start - WINDOW + jnp.arange(span, dtype=jnp.int32)
        inside = (jnp.abs(qpos[:, None] - kpos[None, :]) <= WINDOW) & (kpos[None, :] >= 0) & (kpos[None, :] < LENGTH)
        scores = jnp.where(inside[None], scores, -1e+30)
        top = lax.optimization_barrier(jnp.max(scores, axis=-1, keepdims=True))
        probs = jnp.exp(scores - top)
        denom = lax.optimization_barrier(jnp.sum(probs, axis=-1))
        rounded = lax.optimization_barrier(probs.astype(jnp.bfloat16)).astype(jnp.float32)
        out = jnp.einsum('hrk,khd->rhd', rounded, vblock) / jnp.transpose(denom)[:, :, None]
        return out.reshape(ROWS, D).astype(jnp.bfloat16)
    blocks = lax.map(block, jnp.arange(N_SEQ, dtype=jnp.int32))
    return blocks.reshape(LENGTH, D)

def reference(x_fwd, x_rev, gain, w_qkv):
    att_fwd = strand_attention(x_fwd, gain, w_qkv).astype(jnp.float32)
    att_rev = strand_attention(x_rev, gain, w_qkv).astype(jnp.float32)
    y_fwd = (att_fwd + att_rev[::-1, ::-1]).astype(jnp.bfloat16)
    y_rev = (att_rev + att_fwd[::-1, ::-1]).astype(jnp.bfloat16)
    return (y_fwd, y_rev)
```

```python
import functools

import jax
import jax.numpy as jnp
from jax import lax
from jax.experimental import pallas as pl
from jax.experimental.pallas import tpu as pltpu
from jax.sharding import PartitionSpec as P

HEADS = 16
WINDOW = 512
LOG2E = 1.4426950408889634
NEG = -1e30
VMEM_LIMIT = 56 * 1024 * 1024


def project_kernel(n_parts, rows, q_blocks, scale, *refs):
    x_refs = refs[:n_parts]
    gain_ref, w_ref, out_ref, hn_ref = refs[n_parts:]
    j = pl.program_id(0)

    @pl.when(j == 0)
    def _():
        g = gain_ref[...].astype(jnp.float32)
        for n, x_ref in enumerate(x_refs):
            xf = x_ref[...].astype(jnp.float32)
            meansq = jnp.mean(xf * xf, axis=-1, keepdims=True)
            hn = xf * lax.rsqrt(meansq + 1e-6) * g
            hn_ref[n * rows : (n + 1) * rows, :] = hn.astype(jnp.bfloat16)

    acc = jnp.dot(hn_ref[...], w_ref[...], preferred_element_type=jnp.float32)
    if q_blocks:
        acc = acc * jnp.where(j < q_blocks, scale, 1.0)
    out_ref[...] = acc.astype(jnp.bfloat16)


def project(xs, gain, w, first, block, scale):
    rows, width = xs[0].shape
    n = len(xs)
    columns = w.shape[1] - first
    off = first // block
    q_blocks = max(0, (width - first) // block)
    return pl.pallas_call(
        functools.partial(project_kernel, n, rows, q_blocks, scale),
        out_shape=jax.ShapeDtypeStruct((n * rows, columns), jnp.bfloat16),
        grid=(columns // block,),
        in_specs=[pl.BlockSpec((rows, width), lambda j: (0, 0))] * n
        + [
            pl.BlockSpec((1, width), lambda j: (0, 0)),
            pl.BlockSpec((width, block), lambda j: (0, off + j)),
        ],
        out_specs=pl.BlockSpec((n * rows, block), lambda j: (0, j)),
        scratch_shapes=[pltpu.VMEM((n * rows, width), jnp.bfloat16)],
        compiler_params=pltpu.CompilerParams(vmem_limit_bytes=VMEM_LIMIT),
        cost_estimate=pl.CostEstimate(
            flops=2 * n * rows * width * columns,
            bytes_accessed=2 * (n * rows * (width + columns) + width * columns),
            transcendentals=0,
        ),
        name="project",
    )(*xs, gain, w)


def exchange_matrix(n):
    r = lax.broadcasted_iota(jnp.int32, (n, n), 0)
    c = lax.broadcasted_iota(jnp.int32, (n, n), 1)
    return (r + c == n - 1).astype(jnp.bfloat16)


def flipped(block):
    rows, columns = block.shape
    half = rows // 2
    t = jnp.dot(block, exchange_matrix(columns), preferred_element_type=jnp.float32)
    t = t.astype(jnp.bfloat16)
    ex = exchange_matrix(half)
    top = jnp.dot(ex, t[half:], preferred_element_type=jnp.float32)
    bottom = jnp.dot(ex, t[:half], preferred_element_type=jnp.float32)
    return jnp.concatenate([top, bottom], axis=0)


def attention_kernel(tile, combine, valid_ref, q_ref, kl_ref, ko_ref, kr_ref, vl_ref, vo_ref, vr_ref, *refs):
    if combine:
        near_ref, out_ref, kbuf, vbuf = refs
    else:
        out_ref, kbuf, vbuf = refs
    rows, width = q_ref.shape
    head = width // 2
    has_left = valid_ref[0] > 0
    has_right = valid_ref[1] > 0
    kbuf[:rows] = jnp.where(has_left, kl_ref[...], ko_ref[...])
    kbuf[rows : 2 * rows] = ko_ref[...]
    kbuf[2 * rows :] = jnp.where(has_right, kr_ref[...], ko_ref[...])
    ones = jnp.ones((rows, width), jnp.bfloat16)
    none = jnp.zeros((rows, width), jnp.bfloat16)
    vbuf[:rows, :width] = jnp.where(has_left, vl_ref[...], none)
    vbuf[:rows, width:] = jnp.where(has_left, ones, none)
    vbuf[rows : 2 * rows, :width] = vo_ref[...]
    vbuf[rows : 2 * rows, width:] = ones
    vbuf[2 * rows :, :width] = jnp.where(has_right, vr_ref[...], none)
    vbuf[2 * rows :, width:] = jnp.where(has_right, ones, none)

    span = tile + 2 * WINDOW
    r = lax.broadcasted_iota(jnp.int32, (tile, tile), 0)
    c = lax.broadcasted_iota(jnp.int32, (tile, tile), 1)
    low = c >= r
    high = c <= r
    lane = lax.broadcasted_iota(jnp.int32, (tile, width), 1)
    pieces = []
    for t in range(rows // tile):
        q = q_ref[t * tile : (t + 1) * tile, :]
        keys = kbuf[t * tile : t * tile + span, :]
        values = vbuf[t * tile : t * tile + span, :]
        outs = []
        for h in range(2):
            mine = (lane < head) if h == 0 else (lane >= head)
            qh = jnp.where(mine, q, jnp.zeros_like(q))
            s = lax.dot_general(
                qh, keys, (((1,), (1,)), ((), ())), preferred_element_type=jnp.float32
            )
            s_low = jnp.where(low, s[:, :tile], NEG)
            s_mid = s[:, tile : 2 * WINDOW]
            s_high = jnp.where(high, s[:, 2 * WINDOW :], NEG)
            s = jnp.concatenate([s_low, s_mid, s_high], axis=1)
            top = jnp.max(s, axis=-1, keepdims=True)
            p = jnp.exp2(s - top).astype(jnp.bfloat16)
            o = jnp.dot(p, values, preferred_element_type=jnp.float32)
            outs.append(o[:, :width] / o[:, width:])
        pieces.append(jnp.where(lane < head, outs[0], outs[1]).astype(jnp.bfloat16))
    a = jnp.concatenate(pieces, axis=0)
    if combine:
        out_ref[...] = (near_ref[...].astype(jnp.float32) + flipped(a)).astype(jnp.bfloat16)
    else:
        out_ref[...] = a


def attention(own, halo, valid, first, count, near=None):
    rows = own.shape[0]
    width = own.shape[1] // 3
    pw = 2 * (width // HEADS)
    n = width // pw
    f = first

    def spec(row, col):
        return pl.BlockSpec((rows, pw), lambda g: (row, col + f + g))

    operands = [valid, own, halo, own, halo, halo, own, halo]
    in_specs = [
        pl.BlockSpec(memory_space=pltpu.SMEM),
        spec(0, 0),
        spec(0, 0),
        spec(0, n),
        spec(1, 0),
        spec(0, n),
        spec(0, 2 * n),
        spec(1, n),
    ]
    if near is None:
        out_spec = pl.BlockSpec((rows, pw), lambda g: (0, g))
    else:
        operands.append(near)
        in_specs.append(pl.BlockSpec((rows, pw), lambda g: (0, n - 1 - f - g)))
        out_spec = pl.BlockSpec((rows, pw), lambda g: (0, count - 1 - g))
    return pl.pallas_call(
        functools.partial(attention_kernel, min(256, rows), near is not None),
        out_shape=jax.ShapeDtypeStruct((rows, count * pw), jnp.bfloat16),
        grid=(count,),
        in_specs=in_specs,
        out_specs=out_spec,
        scratch_shapes=[
            pltpu.VMEM((rows + 2 * WINDOW, pw), jnp.bfloat16),
            pltpu.VMEM((rows + 2 * WINDOW, 2 * pw), jnp.bfloat16),
        ],
        compiler_params=pltpu.CompilerParams(vmem_limit_bytes=VMEM_LIMIT),
        cost_estimate=pl.CostEstimate(
            flops=16 * count * rows * (256 + 2 * WINDOW) * 2 * pw,
            bytes_accessed=16 * count * rows * pw,
            transcendentals=2 * count * rows * (256 + 2 * WINDOW),
        ),
        name="attention",
    )(*operands)


def finish_kernel(n, *refs):
    mine, moved, (fwd_ref, rev_ref) = refs[:n], refs[n : 2 * n], refs[2 * n :]
    width = mine[0].shape[1]
    for k in range(n):
        fwd_ref[:, (n - 1 - k) * width : (n - k) * width] = mine[k][...]
        rev_ref[:, k * width : (k + 1) * width] = flipped(moved[k][...]).astype(jnp.bfloat16)


def finish(mine, moved):
    rows = mine[0].shape[0]
    n = len(mine)
    width = sum(m.shape[1] for m in mine)
    out = jax.ShapeDtypeStruct((rows, width), jnp.bfloat16)
    return pl.pallas_call(
        functools.partial(finish_kernel, n),
        out_shape=(out, out),
        compiler_params=pltpu.CompilerParams(vmem_limit_bytes=VMEM_LIMIT),
        cost_estimate=pl.CostEstimate(
            flops=2 * rows * width * 512, bytes_accessed=8 * rows * width, transcendentals=0
        ),
        name="finish",
    )(*mine, *moved)


def per_device(x_fwd, x_rev, gain, w_qkv):
    count = lax.axis_size("seq")
    index = lax.axis_index("seq")
    width = x_fwd.shape[1]
    scale = (width // HEADS) ** (-0.5) * LOG2E
    gain = gain.reshape(1, width)
    mirror = [(i, count - 1 - i) for i in range(count)]
    up = [(i, i + 1) for i in range(count - 1)]
    down = [(i + 1, i) for i in range(count - 1)]

    has_prev = (index > 0).astype(jnp.int32)
    has_next = (index < count - 1).astype(jnp.int32)
    valid_f = jnp.stack([has_prev, has_next])
    valid_r = jnp.stack([has_next, has_prev])

    r_own = lax.ppermute(x_rev, "seq", mirror)
    f_left = lax.ppermute(x_fwd, "seq", up)
    f_right = lax.ppermute(x_fwd, "seq", down)
    r_left = lax.ppermute(r_own, "seq", down)
    r_right = lax.ppermute(r_own, "seq", up)

    pairs = HEADS // 2
    f_qkv = project([x_fwd], gain, w_qkv, 0, 512, scale)
    f_halo = project([f_left, f_right], gain, w_qkv, width, 512, scale)
    a_f = attention(f_qkv, f_halo, valid_f, 0, pairs)

    r_qkv = project([r_own], gain, w_qkv, 0, 512, scale)
    r_halo = project([r_left, r_right], gain, w_qkv, width, 512, scale)
    steps = 4
    each = pairs // steps
    mine, moved = [], []
    for k in range(steps):
        if k >= 2:
            moved[k - 2], r_qkv = lax.optimization_barrier((moved[k - 2], r_qkv))
        y = attention(r_qkv, r_halo, valid_r, k * each, each, near=a_f)
        mine.append(y)
        moved.append(lax.ppermute(y, "seq", mirror))
    return finish(mine, moved)


def solution(mesh):
    in_specs = (P(("dp", "seq"), None), P(("dp", "seq"), None), P(), P())
    out_specs = (P(("dp", "seq"), None), P(("dp", "seq"), None))
    return jax.shard_map(
        per_device, mesh=mesh, in_specs=in_specs, out_specs=out_specs, check_vma=False
    )
```

```python
import functools

import jax
import jax.numpy as jnp
from jax import lax
from jax.experimental import pallas as pl
from jax.experimental.pallas import tpu as pltpu
from jax.sharding import PartitionSpec as P

HEADS = 16
WINDOW = 512
LOG2E = 1.4426950408889634
NEG = -1e30
VMEM_LIMIT = 64 * 1024 * 1024 - 256 * 1024
CHUNKS = (2, 2, 2, 2)


def after(x, *others):
    return lax.optimization_barrier((x, *others))[0]


def exchange_matrix(n):
    r = lax.broadcasted_iota(jnp.int32, (n, n), 0)
    c = lax.broadcasted_iota(jnp.int32, (n, n), 1)
    return (r + c == n - 1).astype(jnp.bfloat16)


def normed(x, gain):
    xf = x.astype(jnp.float32)
    meansq = jnp.mean(xf * xf, axis=-1, keepdims=True)
    return (xf * lax.rsqrt(meansq + 1e-6) * gain.astype(jnp.float32)).astype(jnp.bfloat16)


def product(a, b, scale=None):
    out = jnp.dot(a, b, preferred_element_type=jnp.float32)
    if scale is not None:
        out = out * scale
    return out.astype(jnp.bfloat16)


def attention_kernel(tile, parts, mirrored, combine, valid_ref, q_ref, *refs):
    k_refs, v_refs = refs[:parts], refs[parts : 2 * parts]
    refs = refs[2 * parts :]
    if combine:
        near_ref, out_ref, kbuf, vbuf = refs
    else:
        out_ref, kbuf, vbuf = refs
    rows, width = q_ref.shape
    head = width // 2
    has = (valid_ref[0] > 0, valid_ref[1] > 0)
    each = parts // 3
    size = rows // each
    ones = jnp.ones((size, width), jnp.bfloat16)
    none = jnp.zeros((size, width), jnp.bfloat16)
    for n in range(parts):
        at = slice(n * size, (n + 1) * size)
        side = n // each
        if side == 1:
            kbuf[at] = k_refs[n][...]
            vbuf[at, :width] = v_refs[n][...]
            vbuf[at, width:] = ones
        else:
            there = has[side // 2]
            kbuf[at] = jnp.where(there, k_refs[n][...], k_refs[each][...])
            vbuf[at, :width] = jnp.where(there, v_refs[n][...], none)
            vbuf[at, width:] = jnp.where(there, ones, none)

    span = tile + 2 * WINDOW
    r = lax.broadcasted_iota(jnp.int32, (tile, tile), 0)
    c = lax.broadcasted_iota(jnp.int32, (tile, tile), 1)
    if mirrored:
        r = tile - 1 - r
    low = c >= r
    high = c <= r
    lane = lax.broadcasted_iota(jnp.int32, (tile, width), 1)
    tiles = rows // tile
    for t in range(tiles):
        here = slice(t * tile, (t + 1) * tile)
        q = q_ref[here, :]
        first = (tiles - 1 - t if mirrored else t) * tile
        keys = kbuf[first : first + span, :]
        values = vbuf[first : first + span, :]
        outs = []
        for h in range(2):
            mine = (lane < head) if h == 0 else (lane >= head)
            qh = jnp.where(mine, q, jnp.zeros_like(q))
            s = lax.dot_general(
                qh, keys, (((1,), (1,)), ((), ())), preferred_element_type=jnp.float32
            )
            s_low = jnp.where(low, s[:, :tile], NEG)
            s_mid = s[:, tile : 2 * WINDOW]
            s_high = jnp.where(high, s[:, 2 * WINDOW :], NEG)
            s = jnp.concatenate([s_low, s_mid, s_high], axis=1)
            top = jnp.max(s, axis=-1, keepdims=True)
            p = jnp.exp2(s - top).astype(jnp.bfloat16)
            o = jnp.dot(p, values, preferred_element_type=jnp.float32)
            outs.append(o[:, :width] / o[:, width:])
        if mirrored:
            outs = outs[::-1]
        a = jnp.where(lane < head, outs[0], outs[1]).astype(jnp.bfloat16)
        if combine:
            a = (near_ref[here, :].astype(jnp.float32) + a.astype(jnp.float32)).astype(jnp.bfloat16)
        out_ref[here, :] = a


def attention(q, kvs, valid, first, count, near=None):
    rows, width = q.shape
    pw = 2 * (width // HEADS)
    n = width // pw
    f = first
    mirrored = near is not None
    parts = len(kvs)
    size = 3 * rows // parts

    def at(g):
        return n - 1 - f - g if mirrored else f + g

    in_specs = [pl.BlockSpec(memory_space=pltpu.SMEM), pl.BlockSpec((rows, pw), lambda g: (0, at(g)))]
    in_specs += [pl.BlockSpec((size, pw), lambda g: (0, at(g)))] * parts
    in_specs += [pl.BlockSpec((size, pw), lambda g: (0, n + f + g))] * parts
    operands = [valid, q, *kvs, *kvs]
    out_spec = pl.BlockSpec((rows, pw), lambda g: (0, g))
    if mirrored:
        operands.append(near)
        in_specs.append(out_spec)
    return pl.pallas_call(
        functools.partial(attention_kernel, min(256, rows), parts, mirrored, mirrored),
        out_shape=jax.ShapeDtypeStruct((rows, count * pw), jnp.bfloat16),
        grid=(count,),
        in_specs=in_specs,
        out_specs=out_spec,
        scratch_shapes=[
            pltpu.VMEM((rows + 2 * WINDOW, pw), jnp.bfloat16),
            pltpu.VMEM((rows + 2 * WINDOW, 2 * pw), jnp.bfloat16),
        ],
        compiler_params=pltpu.CompilerParams(vmem_limit_bytes=VMEM_LIMIT),
        cost_estimate=pl.CostEstimate(
            flops=16 * count * rows * (256 + 2 * WINDOW) * 2 * pw // 20,
            bytes_accessed=16 * count * rows * pw // 20,
            transcendentals=0,
        ),
        name="attention_mirrored" if mirrored else "attention",
    )(*operands)


def finish_kernel(mine_ref, moved_ref, *refs):
    fwd_ref, rev_ref = refs[-2:]
    fwd_ref[...] = mine_ref[...]
    rows, width = moved_ref.shape
    half = rows // 2
    t = jnp.dot(moved_ref[...], exchange_matrix(width), preferred_element_type=jnp.float32)
    t = t.astype(jnp.bfloat16)
    ex = exchange_matrix(half)
    rev_ref[:half] = jnp.dot(ex, t[half:], preferred_element_type=jnp.float32).astype(jnp.bfloat16)
    rev_ref[half:] = jnp.dot(ex, t[:half], preferred_element_type=jnp.float32).astype(jnp.bfloat16)


def finish(mine, moved, first, width, held):
    rows, piece = mine.shape
    pw = 2 * (width // HEADS)
    n = width // pw
    f = first
    out = jax.ShapeDtypeStruct((rows, width), jnp.bfloat16)
    block = pl.BlockSpec((rows, pw), lambda g: (0, g))
    held = [] if held is None else list(held)
    return pl.pallas_call(
        finish_kernel,
        out_shape=(out, out),
        grid=(piece // pw,),
        in_specs=[block, block] + [pl.BlockSpec(memory_space=pl.ANY)] * len(held),
        out_specs=(
            pl.BlockSpec((rows, pw), lambda g: (0, f + g)),
            pl.BlockSpec((rows, pw), lambda g: (0, n - 1 - f - g)),
        ),
        input_output_aliases={2: 0, 3: 1} if held else {},
        compiler_params=pltpu.CompilerParams(vmem_limit_bytes=VMEM_LIMIT),
        cost_estimate=pl.CostEstimate(
            flops=2 * rows * piece * 512, bytes_accessed=8 * rows * piece, transcendentals=0
        ),
        name="finish",
    )(mine, moved, *held)


def per_device(x_fwd, x_rev, gain, w_qkv):
    count = lax.axis_size("seq")
    index = lax.axis_index("seq")
    rows, width = x_fwd.shape
    half = rows // 2
    scale = (width // HEADS) ** (-0.5) * LOG2E
    mirror = [(i, count - 1 - i) for i in range(count)]
    up = [(i, i + 1) for i in range(count - 1)]
    down = [(i + 1, i) for i in range(count - 1)]

    def send(x, pairs):
        return lax.ppermute(x, "seq", pairs)

    has_prev = (index > 0).astype(jnp.int32)
    has_next = (index < count - 1).astype(jnp.int32)
    valid_f = jnp.stack([has_prev, has_next])
    valid_r = jnp.stack([has_next, has_prev])

    hn_a = normed(x_rev[:half], gain)
    hn_b = normed(x_rev[half:], gain)
    r_a = send(hn_a, mirror)
    r_b = send(hn_b, mirror)
    hn_f = normed(after(x_fwd, hn_a, hn_b), gain)
    f_left = send(hn_f, up)
    f_right = send(hn_f, down)

    w_q = w_qkv[:, :width]
    w_kv = w_qkv[:, width:]
    w_v_mirrored = product(w_qkv[:, 2 * width :], exchange_matrix(width))
    w_r = jnp.concatenate([w_qkv[:, width : 2 * width], w_v_mirrored], axis=1)
    f_q = product(hn_f, w_q, scale)
    f_own = product(hn_f, w_kv)

    r_a = after(r_a, f_left, f_right)
    r_left_a = send(r_a, down)
    r_right_a = send(r_a, up)
    f_kv = [product(f_left, w_kv), f_own, product(f_right, w_kv)]

    firsts = [sum(CHUNKS[:k]) for k in range(len(CHUNKS))]
    a_f = []
    valid_f = after(valid_f, r_a)
    a_f.append(attention(f_q, f_kv, valid_f, firsts[0], CHUNKS[0]))
    r_own_a = product(after(r_a, a_f[0]), w_r)
    valid_f = after(valid_f, r_own_a)
    a_f.append(attention(f_q, f_kv, valid_f, firsts[1], CHUNKS[1]))

    r_b = after(r_b, a_f[1])
    r_left_b = send(r_b, down)
    r_right_b = send(r_b, up)
    valid_f = after(valid_f, r_b)
    a_f.append(attention(f_q, f_kv, valid_f, firsts[2], CHUNKS[2]))
    r_b_own = after(r_b, a_f[2])
    r_own_b = product(r_b_own, w_r)
    reverse = exchange_matrix(rows)
    r_q = product(product(reverse, jnp.concatenate([r_a, r_b_own], axis=0)), w_q, scale)
    r_left_a = after(r_left_a, r_q)
    r_kv_left_a = product(r_left_a, w_r)
    r_kv_right_a = product(after(r_right_a, r_left_a), w_r)
    r_left_b = after(r_left_b, r_kv_left_a, r_kv_right_a)
    r_kv = [
        r_kv_left_a,
        product(r_left_b, w_r),
        r_own_a,
        r_own_b,
        r_kv_right_a,
        product(after(r_right_b, r_left_b), w_r),
    ]

    mine, moved, held = [], [], None
    for k in range(len(CHUNKS)):
        if k >= 2:
            moved[k - 2], valid_r = lax.optimization_barrier((moved[k - 2], valid_r))
        if k == len(a_f):
            valid_f = after(valid_f, mine[k - 2])
            a_f.append(attention(f_q, f_kv, valid_f, firsts[k], CHUNKS[k]))
        y = attention(r_q, r_kv, valid_r, firsts[k], CHUNKS[k], near=a_f[k])
        valid_r = after(valid_r, y)
        mine.append(y)
        moved.append(send(y, mirror))
    for k in range(len(CHUNKS)):
        held = finish(mine[k], moved[k], firsts[k], width, held)
    return held


def solution(mesh):
    in_specs = (P(("dp", "seq"), None), P(("dp", "seq"), None), P(), P())
    out_specs = (P(("dp", "seq"), None), P(("dp", "seq"), None))
    return jax.shard_map(
        per_device, mesh=mesh, in_specs=in_specs, out_specs=out_specs, check_vma=False
    )
```

```python
import functools

import jax
import jax.numpy as jnp
from jax import lax
from jax.experimental import pallas as pl
from jax.experimental.pallas import tpu as pltpu
from jax.sharding import PartitionSpec as P

HEADS = 16
WINDOW = 512
LOG2E = 1.4426950408889634
NEG = -1e30
SMALL = pl.CostEstimate(flops=1, bytes_accessed=1, transcendentals=0)
VMEM_LIMIT = 64 * 1024 * 1024 - 256 * 1024
A_CHUNKS = (4, 4)
CHUNKS = (2, 2, 2, 2)
EIGHTHS = ()


def after(x, *others):
    return lax.optimization_barrier((x, *others))[0]


def exchange_matrix(n):
    r = lax.broadcasted_iota(jnp.int32, (n, n), 0)
    c = lax.broadcasted_iota(jnp.int32, (n, n), 1)
    return (r + c == n - 1).astype(jnp.bfloat16)


def rows_reversed(x, out_ref):
    half = x.shape[0] // 2
    ex = exchange_matrix(half)
    out_ref[:half] = jnp.dot(ex, x[half:], preferred_element_type=jnp.float32).astype(out_ref.dtype)
    out_ref[half:] = jnp.dot(ex, x[:half], preferred_element_type=jnp.float32).astype(out_ref.dtype)


def columns_reversed(x, out_ref):
    width = x.shape[1]
    size = min(256, width)
    ex = exchange_matrix(size)
    for n in range(width // size):
        t = jnp.dot(x[:, n * size : (n + 1) * size], ex, preferred_element_type=jnp.float32)
        out_ref[:, width - (n + 1) * size : width - n * size] = t.astype(out_ref.dtype)


def project_kernel(scale, mirrored, with_q, n, *refs):
    x_refs = refs[:n]
    gain_ref, w_ref = refs[n : n + 2]
    refs = refs[n + 2 :]
    if with_q:
        q_ref, kv_ref, hn_ref, turned_ref = refs
    else:
        kv_ref, hn_ref, turned_ref = refs
    j = pl.program_id(0)
    rows = x_refs[0].shape[0]

    @pl.when(j == 0)
    def _():
        for m in range(n):
            xf = x_refs[m][...].astype(jnp.float32)
            meansq = jnp.mean(xf * xf, axis=-1, keepdims=True)
            hn = xf * lax.rsqrt(meansq + 1e-6) * gain_ref[...].astype(jnp.float32)
            hn_ref[m * rows : (m + 1) * rows] = hn.astype(jnp.bfloat16)

    def product(h):
        return jnp.dot(h, w_ref[...], preferred_element_type=jnp.float32)

    first = 1 if with_q else 0
    if with_q:

        @pl.when(j == 0)
        def _():
            if mirrored:
                rows_reversed(hn_ref[:rows], turned_ref)
                q_ref[...] = (product(turned_ref[...]) * scale).astype(jnp.bfloat16)
            else:
                q_ref[...] = (product(hn_ref[:rows]) * scale).astype(jnp.bfloat16)

    @pl.when(j == first)
    def _():
        kv_ref[...] = product(hn_ref[...]).astype(jnp.bfloat16)

    @pl.when(j == first + 1)
    def _():
        v = product(hn_ref[...]).astype(jnp.bfloat16)
        if mirrored:
            columns_reversed(v, kv_ref)
        else:
            kv_ref[...] = v


def project(xs, gain, w, scale, mirrored, with_q):
    rows, width = xs[0].shape
    n = len(xs)
    first = 1 if with_q else 0
    kv = jax.ShapeDtypeStruct((n * rows, 2 * width), jnp.bfloat16)
    kv_spec = pl.BlockSpec((n * rows, width), lambda j: (0, jnp.maximum(j - first, 0)))
    q = jax.ShapeDtypeStruct((rows, width), jnp.bfloat16)
    q_spec = pl.BlockSpec((rows, width), lambda j: (0, 0))
    return pl.pallas_call(
        functools.partial(project_kernel, scale, mirrored, with_q, n),
        out_shape=(q, kv) if with_q else kv,
        grid=(2 + first,),
        in_specs=[pl.BlockSpec((rows, width), lambda j: (0, 0))] * n
        + [
            pl.BlockSpec((1, width), lambda j: (0, 0)),
            pl.BlockSpec((width, width), lambda j: (0, j + 1 - first)),
        ],
        out_specs=(q_spec, kv_spec) if with_q else kv_spec,
        scratch_shapes=[
            pltpu.VMEM((n * rows, width), jnp.bfloat16),
            pltpu.VMEM((rows, width), jnp.bfloat16),
        ],
        compiler_params=pltpu.CompilerParams(vmem_limit_bytes=VMEM_LIMIT),
        cost_estimate=SMALL,
        name="project",
    )(*xs, gain, w)


def attention_kernel(tile, mirrored, nears, flags_ref, q_ref, ko_ref, ks_ref, kr_ref, vo_ref, vs_ref, vr_ref, *refs):
    near_refs = refs[:nears]
    out_ref, kbuf, vbuf = refs[nears:]
    rows, width = q_ref.shape
    head = width // 2
    sibling_left = flags_ref[0] > 0
    has_remote = flags_ref[1] > 0
    at_s = pl.multiple_of(jnp.where(sibling_left, 0, 2 * rows), rows)
    at_r = pl.multiple_of(jnp.where(sibling_left, 2 * rows, 0), rows)
    ones = jnp.ones((rows, width), jnp.bfloat16)
    none = jnp.zeros((rows, width), jnp.bfloat16)
    kbuf[rows : 2 * rows] = ko_ref[...]
    vbuf[rows : 2 * rows, :width] = vo_ref[...]
    vbuf[rows : 2 * rows, width:] = ones
    kbuf[pl.ds(at_s, rows)] = ks_ref[...]
    vbuf[pl.ds(at_s, rows), :width] = vs_ref[...]
    vbuf[pl.ds(at_s, rows), width:] = ones
    kbuf[pl.ds(at_r, rows)] = jnp.where(has_remote, kr_ref[...], ko_ref[...])
    vbuf[pl.ds(at_r, rows), :width] = jnp.where(has_remote, vr_ref[...], none)
    vbuf[pl.ds(at_r, rows), width:] = jnp.where(has_remote, ones, none)

    span = tile + 2 * WINDOW
    r = lax.broadcasted_iota(jnp.int32, (tile, tile), 0)
    c = lax.broadcasted_iota(jnp.int32, (tile, tile), 1)
    if mirrored:
        r = tile - 1 - r
    low = c >= r
    high = c <= r
    lane = lax.broadcasted_iota(jnp.int32, (tile, width), 1)
    tiles = rows // tile
    for t in range(tiles):
        here = slice(t * tile, (t + 1) * tile)
        q = q_ref[here, :]
        first = (tiles - 1 - t if mirrored else t) * tile
        keys = kbuf[first : first + span, :]
        values = vbuf[first : first + span, :]
        outs = []
        for h in range(2):
            mine = (lane < head) if h == 0 else (lane >= head)
            qh = jnp.where(mine, q, jnp.zeros_like(q))
            s = lax.dot_general(
                qh, keys, (((1,), (1,)), ((), ())), preferred_element_type=jnp.float32
            )
            s_low = jnp.where(low, s[:, :tile], NEG)
            s_mid = s[:, tile : 2 * WINDOW]
            s_high = jnp.where(high, s[:, 2 * WINDOW :], NEG)
            s = jnp.concatenate([s_low, s_mid, s_high], axis=1)
            top = jnp.max(s, axis=-1, keepdims=True)
            p = jnp.exp2(s - top).astype(jnp.bfloat16)
            o = jnp.dot(p, values, preferred_element_type=jnp.float32)
            outs.append(o[:, :width] / o[:, width:])
        if mirrored:
            outs = outs[::-1]
        a = jnp.where(lane < head, outs[0], outs[1]).astype(jnp.bfloat16)
        if nears:
            near = near_refs[0][here, :]
            if nears == 2:
                near = jnp.where(flags_ref[2] > 0, near, near_refs[1][here, :])
            a = (near.astype(jnp.float32) + a.astype(jnp.float32)).astype(jnp.bfloat16)
        out_ref[here, :] = a


def attention(q, chip, remote, flags, first, count, near=(), near_first=0):
    rows, width = q.shape
    pw = 2 * (width // HEADS)
    n = width // pw
    f = first
    mirrored = len(near) > 0

    def keys(row):
        return pl.BlockSpec((rows, pw), lambda g: (row, n - 1 - f - g if mirrored else f + g))

    def values(row):
        return pl.BlockSpec((rows, pw), lambda g: (row, n + f + g))

    near_spec = pl.BlockSpec((rows, pw), lambda g: (0, near_first + g))
    out_spec = pl.BlockSpec((rows, pw), lambda g: (0, g))
    return pl.pallas_call(
        functools.partial(attention_kernel, min(256, rows), mirrored, len(near)),
        out_shape=jax.ShapeDtypeStruct((rows, count * pw), jnp.bfloat16),
        grid=(count,),
        in_specs=[pl.BlockSpec(memory_space=pltpu.SMEM)]
        + [keys(0), keys(0), keys(1), keys(0), values(0), values(1), values(0)]
        + [near_spec] * len(near),
        out_specs=out_spec,
        scratch_shapes=[
            pltpu.VMEM((rows + 2 * WINDOW, pw), jnp.bfloat16),
            pltpu.VMEM((rows + 2 * WINDOW, 2 * pw), jnp.bfloat16),
        ],
        compiler_params=pltpu.CompilerParams(vmem_limit_bytes=VMEM_LIMIT),
        cost_estimate=SMALL,
        name="attention_mirrored" if mirrored else "attention",
    )(flags, q, chip, chip, remote, chip, chip, remote, *near)


def finish_kernel(flags_ref, mine_ref, moved_ref, *refs):
    fwd_ref, rev_ref = refs[-2:]
    fetched = flags_ref[2] > 0
    mine, moved = mine_ref[...], moved_ref[...]
    fwd_ref[...] = jnp.where(fetched, mine, moved)
    t = jnp.where(fetched, moved, mine)
    t = jnp.dot(t, exchange_matrix(t.shape[1]), preferred_element_type=jnp.float32)
    rows_reversed(t.astype(jnp.bfloat16), rev_ref)


def finish(flags, mine, moved, first, width, held):
    rows, piece = mine.shape
    pw = 2 * (width // HEADS)
    n = width // pw
    f = first
    out = jax.ShapeDtypeStruct((rows, width), jnp.bfloat16)
    block = pl.BlockSpec((rows, pw), lambda g: (0, g))
    return pl.pallas_call(
        finish_kernel,
        out_shape=(out, out),
        grid=(piece // pw,),
        in_specs=[pl.BlockSpec(memory_space=pltpu.SMEM), block, block]
        + [pl.BlockSpec(memory_space=pl.ANY)] * len(held),
        out_specs=(
            pl.BlockSpec((rows, pw), lambda g: (0, f + g)),
            pl.BlockSpec((rows, pw), lambda g: (0, n - 1 - f - g)),
        ),
        input_output_aliases={3: 0, 4: 1} if held else {},
        compiler_params=pltpu.CompilerParams(vmem_limit_bytes=VMEM_LIMIT),
        cost_estimate=SMALL,
        name="finish",
    )(flags, mine, moved, *held)


def routes(count):
    fetch = [i * 8 // count in EIGHTHS for i in range(count)]
    place = [count - 1 - i if fetch[i] else i for i in range(count)]
    pairs, home, has = [], [True] * count, [False] * count
    for i in range(count):
        wanted = 2 * place[i] - place[i ^ 1]
        if 0 <= wanted < count:
            has[i] = True
            beside = i - 1 if i % 2 == 0 else i + 1
            if fetch[i] and 0 <= beside < count and fetch[beside]:
                source, home[beside] = beside, False
            else:
                source = wanted
            pairs.append((source, i))
    assert len({s for s, _ in pairs}) == len(pairs)
    for s, i in pairs:
        wanted = 2 * place[i] - place[i ^ 1]
        assert (s if home[s] else place[s]) == wanted
    return fetch, place, pairs, home, has


def per_device(x_fwd, x_rev, gain, w_qkv):
    count = lax.axis_size("seq")
    index = lax.axis_index("seq")
    rows, width = x_fwd.shape
    scale = (width // HEADS) ** (-0.5) * LOG2E
    gain = gain.reshape(1, width)
    fetch, place, s_pairs, home, s_has = routes(count)
    sibling = [(i, i ^ 1) for i in range(count)]
    beside = [(i, i - 1 if i % 2 == 0 else i + 1) for i in range(1, count - 1)]
    mirror = [(i, count - 1 - i) for i in range(count)]

    def pick(values):
        return jnp.asarray(values, jnp.int32)[index]

    def send(x, pairs):
        return lax.ppermute(x, "seq", pairs)

    f_flags = jnp.stack([index % 2, (index > 0) & (index < count - 1), index]).astype(jnp.int32)
    s_flags = jnp.stack([pick([place[i ^ 1] < place[i] for i in range(count)]), pick(s_has), pick(fetch)])

    f_x = send(x_fwd, beside)
    f_y = send(x_fwd, sibling)
    own = x_rev
    payload = x_rev
    if any(fetch):
        swapped = send(x_rev, [m for m in mirror if fetch[m[0]]])
        own = jnp.where(pick(fetch) > 0, swapped, x_rev)
        payload = jnp.where(pick(home) > 0, x_rev, swapped)
    f_q, f_chip = project([x_fwd, f_y], gain, w_qkv, scale, False, True)

    payload = after(payload, f_x, f_q)
    s_x = send(payload, s_pairs)
    s_y = send(after(own, payload), sibling)
    f_rem = project([after(f_x, payload)], gain, w_qkv, scale, False, False)

    a_firsts = [sum(A_CHUNKS[:k]) for k in range(len(A_CHUNKS))]
    firsts = [sum(CHUNKS[:k]) for k in range(len(CHUNKS))]
    a_f, a_moved = [], []
    for k in range(len(A_CHUNKS)):
        if k == 1:
            s_q, s_chip = project([own, after(s_y, a_f[0])], gain, w_qkv, scale, True, True)
            f_flags = after(f_flags, s_chip)
        a = attention(f_q, f_chip, f_rem, f_flags, a_firsts[k], A_CHUNKS[k])
        f_flags = after(f_flags, a)
        a_f.append(a)
        if not all(fetch):
            a_moved.append(send(a, [m for m in mirror if not fetch[m[0]]]))
    s_rem = project([after(s_x, a_f[-1])], gain, w_qkv, scale, True, False)

    mine, moved = [], []
    for k in range(len(CHUNKS)):
        at = max(m for m in range(len(A_CHUNKS)) if a_firsts[m] <= firsts[k])
        near = [a_f[at]] if any(fetch) else []
        near += [a_moved[at]] if not all(fetch) else []
        if k >= 2:
            moved[k - 2], s_flags = lax.optimization_barrier((moved[k - 2], s_flags))
        y = attention(s_q, s_chip, s_rem, s_flags, firsts[k], CHUNKS[k], near, firsts[k] - a_firsts[at])
        s_flags = after(s_flags, y)
        mine.append(y)
        moved.append(send(y, mirror))
    held = ()
    for k in range(len(CHUNKS)):
        held = finish(s_flags, mine[k], moved[k], firsts[k], width, held)
    return held


def solution(mesh):
    in_specs = (P(("dp", "seq"), None), P(("dp", "seq"), None), P(), P())
    out_specs = (P(("dp", "seq"), None), P(("dp", "seq"), None))
    return jax.shard_map(
        per_device, mesh=mesh, in_specs=in_specs, out_specs=out_specs, check_vma=False
    )
```

```python
import functools

import jax
import jax.numpy as jnp
from jax import lax
from jax.experimental import pallas as pl
from jax.experimental.pallas import tpu as pltpu
from jax.sharding import PartitionSpec as P

HEADS = 16
WINDOW = 512
LOG2E = 1.4426950408889634
NEG = -1e30
SMALL = pl.CostEstimate(flops=1, bytes_accessed=1, transcendentals=0)
VMEM_LIMIT = 64 * 1024 * 1024 - 256 * 1024
CHUNKS = (2, 2, 2, 2)


def after(x, *others):
    return lax.optimization_barrier((x, *others))[0]


def exchange_matrix(n):
    r = lax.broadcasted_iota(jnp.int32, (n, n), 0)
    c = lax.broadcasted_iota(jnp.int32, (n, n), 1)
    return (r + c == n - 1).astype(jnp.bfloat16)


def rows_reversed(x, out_ref):
    half = x.shape[0] // 2
    ex = exchange_matrix(half)
    out_ref[:half] = jnp.dot(ex, x[half:], preferred_element_type=jnp.float32).astype(out_ref.dtype)
    out_ref[half:] = jnp.dot(ex, x[:half], preferred_element_type=jnp.float32).astype(out_ref.dtype)


def columns_reversed(x, out_ref):
    width = x.shape[1]
    size = min(256, width)
    ex = exchange_matrix(size)
    for n in range(width // size):
        t = jnp.dot(x[:, n * size : (n + 1) * size], ex, preferred_element_type=jnp.float32)
        out_ref[:, width - (n + 1) * size : width - n * size] = t.astype(out_ref.dtype)


def project_kernel(scale, mirrored, with_q, n, *refs):
    x_refs = refs[:n]
    gain_ref, w_ref = refs[n : n + 2]
    refs = refs[n + 2 :]
    if with_q:
        q_ref, kv_ref, hn_ref, turned_ref = refs
    else:
        kv_ref, hn_ref, turned_ref = refs
    j = pl.program_id(0)
    rows = x_refs[0].shape[0]

    @pl.when(j == 0)
    def _():
        for m in range(n):
            xf = x_refs[m][...].astype(jnp.float32)
            meansq = jnp.mean(xf * xf, axis=-1, keepdims=True)
            hn = xf * lax.rsqrt(meansq + 1e-6) * gain_ref[...].astype(jnp.float32)
            hn_ref[m * rows : (m + 1) * rows] = hn.astype(jnp.bfloat16)

    def product(h):
        return jnp.dot(h, w_ref[...], preferred_element_type=jnp.float32)

    first = 1 if with_q else 0
    if with_q:

        @pl.when(j == 0)
        def _():
            if mirrored:
                rows_reversed(hn_ref[:rows], turned_ref)
                q_ref[...] = (product(turned_ref[...]) * scale).astype(jnp.bfloat16)
            else:
                q_ref[...] = (product(hn_ref[:rows]) * scale).astype(jnp.bfloat16)

    @pl.when(j == first)
    def _():
        kv_ref[...] = product(hn_ref[...]).astype(jnp.bfloat16)

    @pl.when(j == first + 1)
    def _():
        v = product(hn_ref[...]).astype(jnp.bfloat16)
        if mirrored:
            columns_reversed(v, kv_ref)
        else:
            kv_ref[...] = v


def project(xs, gain, w, scale, mirrored, with_q, part=0, parts=1):
    rows, width = xs[0].shape
    n = len(xs)
    block = width // parts
    first = 1 if with_q else 0
    kv = jax.ShapeDtypeStruct((n * rows, 2 * block), jnp.bfloat16)
    kv_spec = pl.BlockSpec((n * rows, block), lambda j: (0, jnp.maximum(j - first, 0)))
    q = jax.ShapeDtypeStruct((rows, width), jnp.bfloat16)
    q_spec = pl.BlockSpec((rows, width), lambda j: (0, 0))
    return pl.pallas_call(
        functools.partial(project_kernel, scale, mirrored, with_q, n),
        out_shape=(q, kv) if with_q else kv,
        grid=(2 + first,),
        in_specs=[pl.BlockSpec((rows, width), lambda j: (0, 0))] * n
        + [
            pl.BlockSpec((1, width), lambda j: (0, 0)),
            pl.BlockSpec((width, block), lambda j: (0, parts * (j + 1 - first) + part)),
        ],
        out_specs=(q_spec, kv_spec) if with_q else kv_spec,
        scratch_shapes=[
            pltpu.VMEM((n * rows, width), jnp.bfloat16),
            pltpu.VMEM((rows, width), jnp.bfloat16),
        ],
        compiler_params=pltpu.CompilerParams(vmem_limit_bytes=VMEM_LIMIT),
        cost_estimate=SMALL,
        name="project",
    )(*xs, gain, w)


def attention_kernel(tile, mirrored, flags_ref, q_ref, ko_ref, ks_ref, kr_ref, vo_ref, vs_ref, vr_ref, *refs):
    if mirrored:
        near_ref, out_ref, kbuf, vbuf = refs
    else:
        out_ref, kbuf, vbuf = refs
    rows, width = q_ref.shape
    head = width // 2
    sibling_left = flags_ref[0] > 0
    has_remote = flags_ref[1] > 0
    at_s = pl.multiple_of(jnp.where(sibling_left, 0, 2 * rows), rows)
    at_r = pl.multiple_of(jnp.where(sibling_left, 2 * rows, 0), rows)
    ones = jnp.ones((rows, width), jnp.bfloat16)
    none = jnp.zeros((rows, width), jnp.bfloat16)
    kbuf[rows : 2 * rows] = ko_ref[...]
    vbuf[rows : 2 * rows, :width] = vo_ref[...]
    vbuf[rows : 2 * rows, width:] = ones
    kbuf[pl.ds(at_s, rows)] = ks_ref[...]
    vbuf[pl.ds(at_s, rows), :width] = vs_ref[...]
    vbuf[pl.ds(at_s, rows), width:] = ones
    kbuf[pl.ds(at_r, rows)] = jnp.where(has_remote, kr_ref[...], ko_ref[...])
    vbuf[pl.ds(at_r, rows), :width] = jnp.where(has_remote, vr_ref[...], none)
    vbuf[pl.ds(at_r, rows), width:] = jnp.where(has_remote, ones, none)

    span = tile + 2 * WINDOW
    r = lax.broadcasted_iota(jnp.int32, (tile, tile), 0)
    c = lax.broadcasted_iota(jnp.int32, (tile, tile), 1)
    if mirrored:
        r = tile - 1 - r
    low = c >= r
    high = c <= r
    lane = lax.broadcasted_iota(jnp.int32, (tile, width), 1)
    tiles = rows // tile
    for t in range(tiles):
        here = slice(t * tile, (t + 1) * tile)
        q = q_ref[here, :]
        first = (tiles - 1 - t if mirrored else t) * tile
        keys = kbuf[first : first + span, :]
        values = vbuf[first : first + span, :]
        outs = []
        for h in range(2):
            mine = (lane < head) if h == 0 else (lane >= head)
            qh = jnp.where(mine, q, jnp.zeros_like(q))
            s = lax.dot_general(
                qh, keys, (((1,), (1,)), ((), ())), preferred_element_type=jnp.float32
            )
            s_low = jnp.where(low, s[:, :tile], NEG)
            s_mid = s[:, tile : 2 * WINDOW]
            s_high = jnp.where(high, s[:, 2 * WINDOW :], NEG)
            s = jnp.concatenate([s_low, s_mid, s_high], axis=1)
            top = jnp.max(s, axis=-1, keepdims=True)
            p = jnp.exp2(s - top).astype(jnp.bfloat16)
            o = jnp.dot(p, values, preferred_element_type=jnp.float32)
            outs.append(o[:, :width] / o[:, width:])
        if mirrored:
            outs = outs[::-1]
        a = jnp.where(lane < head, outs[0], outs[1]).astype(jnp.bfloat16)
        if mirrored:
            a = (near_ref[here, :].astype(jnp.float32) + a.astype(jnp.float32)).astype(jnp.bfloat16)
        out_ref[here, :] = a


def attention(q, own, sibling, remote, flags, first, count, base=0, near=None):
    rows, width = q.shape
    pw = 2 * (width // HEADS)
    n = width // pw
    f = first
    mirrored = near is not None

    def key(g):
        return n - 1 - f - g if mirrored else f + g

    def keys(row):
        return pl.BlockSpec((rows, pw), lambda g: (row, key(g)))

    def values(row):
        return pl.BlockSpec((rows, pw), lambda g: (row, n + f + g))

    there = sibling.shape[0] // rows - 1
    held = remote.shape[1] // (2 * pw)
    remote_keys = pl.BlockSpec((rows, pw), lambda g: (0, key(g) - base))
    remote_values = pl.BlockSpec((rows, pw), lambda g: (0, held + f + g - base))
    out_spec = pl.BlockSpec((rows, pw), lambda g: (0, g))
    return pl.pallas_call(
        functools.partial(attention_kernel, min(256, rows), mirrored),
        out_shape=jax.ShapeDtypeStruct((rows, count * pw), jnp.bfloat16),
        grid=(count,),
        in_specs=[pl.BlockSpec(memory_space=pltpu.SMEM)]
        + [keys(0), keys(0), keys(there), remote_keys, values(0), values(there), remote_values]
        + [out_spec] * mirrored,
        out_specs=out_spec,
        scratch_shapes=[
            pltpu.VMEM((rows + 2 * WINDOW, pw), jnp.bfloat16),
            pltpu.VMEM((rows + 2 * WINDOW, 2 * pw), jnp.bfloat16),
        ],
        compiler_params=pltpu.CompilerParams(vmem_limit_bytes=VMEM_LIMIT),
        cost_estimate=pl.CostEstimate(
            flops=16 * count * rows * (256 + 2 * WINDOW) * 2 * pw,
            bytes_accessed=16 * count * rows * pw,
            transcendentals=0,
        ),
        name="attention_mirrored" if mirrored else "attention",
    )(flags, q, own, sibling, remote, own, sibling, remote, *([near] if mirrored else []))


def place_kernel(turned, piece_ref, *refs):
    out_ref = refs[-1]
    if turned:
        t = jnp.dot(piece_ref[...], exchange_matrix(piece_ref.shape[1]), preferred_element_type=jnp.float32)
        rows_reversed(t.astype(jnp.bfloat16), out_ref)
    else:
        out_ref[...] = piece_ref[...]


def place(piece, first, width, held, turned):
    rows, columns = piece.shape
    pw = 2 * (width // HEADS)
    n = width // pw
    f = first
    held = [] if held is None else [held]
    return pl.pallas_call(
        functools.partial(place_kernel, turned),
        out_shape=jax.ShapeDtypeStruct((rows, width), jnp.bfloat16),
        grid=(columns // pw,),
        in_specs=[pl.BlockSpec((rows, pw), lambda g: (0, g))]
        + [pl.BlockSpec(memory_space=pl.ANY)] * len(held),
        out_specs=pl.BlockSpec((rows, pw), lambda g: (0, n - 1 - f - g if turned else f + g)),
        input_output_aliases={1: 0} if held else {},
        compiler_params=pltpu.CompilerParams(vmem_limit_bytes=VMEM_LIMIT),
        cost_estimate=SMALL,
        name="place",
    )(piece, *held)


def per_device(x_fwd, x_rev, gain, w_qkv):
    count = lax.axis_size("seq")
    index = lax.axis_index("seq")
    rows, width = x_fwd.shape
    scale = (width // HEADS) ** (-0.5) * LOG2E
    gain = gain.reshape(1, width)
    sibling = [(i, i ^ 1) for i in range(count)]
    beside = [(i, i - 1 if i % 2 == 0 else i + 1) for i in range(1, count - 1)]
    mirror = [(i, count - 1 - i) for i in range(count)]
    firsts = [sum(CHUNKS[:k]) for k in range(len(CHUNKS))]
    half = HEADS // 4

    def send(x, pairs):
        return lax.ppermute(x, "seq", pairs)

    flags = jnp.stack([index % 2, ((index > 0) & (index < count - 1)).astype(jnp.int32)])

    f_x = send(x_fwd, beside)
    f_y = send(x_fwd, sibling)
    f_q, f_chip = project([x_fwd, f_y], gain, w_qkv, scale, False, True)
    s_q, s_own = project([after(x_rev, f_q)], gain, w_qkv, scale, True, True)
    s_x = send(after(x_rev, s_q), beside)

    s_sib = send(s_own, sibling)
    f_x = after(f_x, s_q)
    a_f, a_moved = [], []
    f_rem = None
    for k in range(len(CHUNKS)):
        if firsts[k] % half == 0:
            f_rem = project([f_x], gain, w_qkv, scale, False, False, firsts[k] // half, 2)
            flags = after(flags, f_rem)
        if k >= 2:
            a_moved[k - 2], flags = lax.optimization_barrier((a_moved[k - 2], flags))
        a = attention(f_q, f_chip, f_chip, f_rem, flags, firsts[k], CHUNKS[k], firsts[k] // half * half)
        flags, f_x = lax.optimization_barrier((flags, f_x, a))[:2]
        a_f.append(a)
        a_moved.append(send(a, mirror))
    s_rem = project([after(s_x, a_f[-1])], gain, w_qkv, scale, True, False)

    mine, moved, fwd, rev = [], [], None, None
    for k in range(len(CHUNKS)):
        if k >= 2:
            moved[k - 2], flags = lax.optimization_barrier((moved[k - 2], flags))
        ahead = min(k + 2, len(CHUNKS) - 1)
        a_moved[ahead], flags = lax.optimization_barrier((a_moved[ahead], flags))
        y = attention(s_q, s_own, s_sib, s_rem, flags, firsts[k], CHUNKS[k], 0, a_moved[k])
        flags = after(flags, y)
        mine.append(y)
        moved.append(send(y, mirror))
    for k in range(len(CHUNKS)):
        rev = place(mine[k], firsts[k], width, rev, True)
    for k in range(len(CHUNKS)):
        fwd = place(after(moved[k], rev), firsts[k], width, fwd, False)
    return fwd, rev


def solution(mesh):
    in_specs = (P(("dp", "seq"), None), P(("dp", "seq"), None), P(), P())
    out_specs = (P(("dp", "seq"), None), P(("dp", "seq"), None))
    return jax.shard_map(
        per_device, mesh=mesh, in_specs=in_specs, out_specs=out_specs, check_vma=False
    )
```

```python
import functools

import jax
import jax.numpy as jnp
from jax import lax
from jax.experimental import pallas as pl
from jax.experimental.pallas import tpu as pltpu
from jax.sharding import PartitionSpec as P

HEADS = 16
WINDOW = 512
LOG2E = 1.4426950408889634
NEG = -1e30
SMALL = pl.CostEstimate(flops=1, bytes_accessed=1, transcendentals=0)
VMEM_LIMIT = 64 * 1024 * 1024 - 256 * 1024
CHUNKS = (2, 3, 3)


def after(x, *others):
    return lax.optimization_barrier((x, *others))[0]


def exchange_matrix(n):
    r = lax.broadcasted_iota(jnp.int32, (n, n), 0)
    c = lax.broadcasted_iota(jnp.int32, (n, n), 1)
    return (r + c == n - 1).astype(jnp.bfloat16)


def rows_reversed(x, out_ref):
    half = x.shape[0] // 2
    ex = exchange_matrix(half)
    out_ref[:half] = jnp.dot(ex, x[half:], preferred_element_type=jnp.float32).astype(out_ref.dtype)
    out_ref[half:] = jnp.dot(ex, x[:half], preferred_element_type=jnp.float32).astype(out_ref.dtype)


def columns_reversed(x, out_ref):
    width = x.shape[1]
    size = min(256, width)
    ex = exchange_matrix(size)
    for n in range(width // size):
        t = jnp.dot(x[:, n * size : (n + 1) * size], ex, preferred_element_type=jnp.float32)
        out_ref[:, width - (n + 1) * size : width - n * size] = t.astype(out_ref.dtype)


def project_kernel(scale, mirrored, with_q, n, *refs):
    x_refs = refs[:n]
    gain_ref, w_ref = refs[n : n + 2]
    refs = refs[n + 2 :]
    if with_q:
        q_ref, kv_ref, hn_ref, turned_ref = refs
    else:
        kv_ref, hn_ref, turned_ref = refs
    j = pl.program_id(0)
    rows = x_refs[0].shape[0]

    @pl.when(j == 0)
    def _():
        for m in range(n):
            xf = x_refs[m][...].astype(jnp.float32)
            meansq = jnp.mean(xf * xf, axis=-1, keepdims=True)
            hn = xf * lax.rsqrt(meansq + 1e-6) * gain_ref[...].astype(jnp.float32)
            hn_ref[m * rows : (m + 1) * rows] = hn.astype(jnp.bfloat16)

    def product(h):
        return jnp.dot(h, w_ref[...], preferred_element_type=jnp.float32)

    first = 1 if with_q else 0
    if with_q:

        @pl.when(j == 0)
        def _():
            if mirrored:
                rows_reversed(hn_ref[:rows], turned_ref)
                q_ref[...] = (product(turned_ref[...]) * scale).astype(jnp.bfloat16)
            else:
                q_ref[...] = (product(hn_ref[:rows]) * scale).astype(jnp.bfloat16)

    @pl.when(j == first)
    def _():
        kv_ref[...] = product(hn_ref[...]).astype(jnp.bfloat16)

    @pl.when(j == first + 1)
    def _():
        v = product(hn_ref[...]).astype(jnp.bfloat16)
        if mirrored:
            columns_reversed(v, kv_ref)
        else:
            kv_ref[...] = v


def project(xs, gain, w, scale, mirrored, with_q, part=0, parts=1):
    rows, width = xs[0].shape
    n = len(xs)
    block = width // parts
    first = 1 if with_q else 0
    kv = jax.ShapeDtypeStruct((n * rows, 2 * block), jnp.bfloat16)
    kv_spec = pl.BlockSpec((n * rows, block), lambda j: (0, jnp.maximum(j - first, 0)))
    q = jax.ShapeDtypeStruct((rows, width), jnp.bfloat16)
    q_spec = pl.BlockSpec((rows, width), lambda j: (0, 0))
    return pl.pallas_call(
        functools.partial(project_kernel, scale, mirrored, with_q, n),
        out_shape=(q, kv) if with_q else kv,
        grid=(2 + first,),
        in_specs=[pl.BlockSpec((rows, width), lambda j: (0, 0))] * n
        + [
            pl.BlockSpec((1, width), lambda j: (0, 0)),
            pl.BlockSpec((width, block), lambda j: (0, parts * (j + 1 - first) + part)),
        ],
        out_specs=(q_spec, kv_spec) if with_q else kv_spec,
        scratch_shapes=[
            pltpu.VMEM((n * rows, width), jnp.bfloat16),
            pltpu.VMEM((rows, width), jnp.bfloat16),
        ],
        compiler_params=pltpu.CompilerParams(vmem_limit_bytes=VMEM_LIMIT),
        cost_estimate=SMALL,
        name="project",
    )(*xs, gain, w)


def attention_kernel(tile, mirrored, flags_ref, q_ref, ko_ref, ks_ref, kr_ref, vo_ref, vs_ref, vr_ref, *refs):
    if mirrored:
        near_ref, out_ref, kbuf, vbuf = refs
    else:
        out_ref, kbuf, vbuf = refs
    rows, width = q_ref.shape
    head = width // 2
    sibling_left = flags_ref[0] > 0
    has_remote = flags_ref[1] > 0
    at_s = pl.multiple_of(jnp.where(sibling_left, 0, 2 * rows), rows)
    at_r = pl.multiple_of(jnp.where(sibling_left, 2 * rows, 0), rows)
    ones = jnp.ones((rows, width), jnp.bfloat16)
    none = jnp.zeros((rows, width), jnp.bfloat16)
    kbuf[rows : 2 * rows] = ko_ref[...]
    vbuf[rows : 2 * rows, :width] = vo_ref[...]
    vbuf[rows : 2 * rows, width:] = ones
    kbuf[pl.ds(at_s, rows)] = ks_ref[...]
    vbuf[pl.ds(at_s, rows), :width] = vs_ref[...]
    vbuf[pl.ds(at_s, rows), width:] = ones
    kbuf[pl.ds(at_r, rows)] = jnp.where(has_remote, kr_ref[...], ko_ref[...])
    vbuf[pl.ds(at_r, rows), :width] = jnp.where(has_remote, vr_ref[...], none)
    vbuf[pl.ds(at_r, rows), width:] = jnp.where(has_remote, ones, none)

    span = tile + 2 * WINDOW
    r = lax.broadcasted_iota(jnp.int32, (tile, tile), 0)
    c = lax.broadcasted_iota(jnp.int32, (tile, tile), 1)
    if mirrored:
        r = tile - 1 - r
    low = c >= r
    high = c <= r
    lane = lax.broadcasted_iota(jnp.int32, (tile, width), 1)
    tiles = rows // tile
    for t in range(tiles):
        here = slice(t * tile, (t + 1) * tile)
        q = q_ref[here, :]
        first = (tiles - 1 - t if mirrored else t) * tile
        keys = kbuf[first : first + span, :]
        values = vbuf[first : first + span, :]
        outs = []
        for h in range(2):
            mine = (lane < head) if h == 0 else (lane >= head)
            qh = jnp.where(mine, q, jnp.zeros_like(q))
            s = lax.dot_general(
                qh, keys, (((1,), (1,)), ((), ())), preferred_element_type=jnp.float32
            )
            s_low = jnp.where(low, s[:, :tile], NEG)
            s_mid = s[:, tile : 2 * WINDOW]
            s_high = jnp.where(high, s[:, 2 * WINDOW :], NEG)
            s = jnp.concatenate([s_low, s_mid, s_high], axis=1)
            top = jnp.max(s, axis=-1, keepdims=True)
            p = jnp.exp2(s - top).astype(jnp.bfloat16)
            o = jnp.dot(p, values, preferred_element_type=jnp.float32)
            outs.append(o[:, :width] / o[:, width:])
        if mirrored:
            outs = outs[::-1]
        a = jnp.where(lane < head, outs[0], outs[1]).astype(jnp.bfloat16)
        if mirrored:
            a = (near_ref[here, :].astype(jnp.float32) + a.astype(jnp.float32)).astype(jnp.bfloat16)
        out_ref[here, :] = a


def attention(q, own, sibling, remote, flags, first, count, near=None):
    rows, width = q.shape
    pw = 2 * (width // HEADS)
    n = width // pw
    f = first
    mirrored = near is not None

    def key(g):
        return n - 1 - f - g if mirrored else f + g

    def keys(row):
        return pl.BlockSpec((rows, pw), lambda g: (row, key(g)))

    def values(row):
        return pl.BlockSpec((rows, pw), lambda g: (row, n + f + g))

    there = sibling.shape[0] // rows - 1
    held = remote.shape[1] // (2 * pw)
    remote_keys = pl.BlockSpec((rows, pw), lambda g: (0, key(g)))
    remote_values = pl.BlockSpec((rows, pw), lambda g: (0, held + f + g))
    out_spec = pl.BlockSpec((rows, pw), lambda g: (0, g))
    return pl.pallas_call(
        functools.partial(attention_kernel, min(256, rows), mirrored),
        out_shape=jax.ShapeDtypeStruct((rows, count * pw), jnp.bfloat16),
        grid=(count,),
        in_specs=[pl.BlockSpec(memory_space=pltpu.SMEM)]
        + [keys(0), keys(0), keys(there), remote_keys, values(0), values(there), remote_values]
        + [out_spec] * mirrored,
        out_specs=out_spec,
        scratch_shapes=[
            pltpu.VMEM((rows + 2 * WINDOW, pw), jnp.bfloat16),
            pltpu.VMEM((rows + 2 * WINDOW, 2 * pw), jnp.bfloat16),
        ],
        compiler_params=pltpu.CompilerParams(vmem_limit_bytes=VMEM_LIMIT),
        cost_estimate=pl.CostEstimate(
            flops=4 * count * rows * (256 + 2 * WINDOW) * 2 * pw,
            bytes_accessed=4 * count * rows * pw,
            transcendentals=0,
        ),
        name="attention_mirrored" if mirrored else "attention",
    )(flags, q, own, sibling, remote, own, sibling, remote, *([near] if mirrored else []))


def place_kernel(turned, piece_ref, *refs):
    out_ref = refs[-1]
    if turned:
        t = jnp.dot(piece_ref[...], exchange_matrix(piece_ref.shape[1]), preferred_element_type=jnp.float32)
        rows_reversed(t.astype(jnp.bfloat16), out_ref)
    else:
        out_ref[...] = piece_ref[...]


def place(piece, first, width, held, turned):
    rows, columns = piece.shape
    pw = 2 * (width // HEADS)
    n = width // pw
    f = first
    held = [] if held is None else [held]
    return pl.pallas_call(
        functools.partial(place_kernel, turned),
        out_shape=jax.ShapeDtypeStruct((rows, width), jnp.bfloat16),
        grid=(columns // pw,),
        in_specs=[pl.BlockSpec((rows, pw), lambda g: (0, g))]
        + [pl.BlockSpec(memory_space=pl.ANY)] * len(held),
        out_specs=pl.BlockSpec((rows, pw), lambda g: (0, n - 1 - f - g if turned else f + g)),
        input_output_aliases={1: 0} if held else {},
        compiler_params=pltpu.CompilerParams(vmem_limit_bytes=VMEM_LIMIT),
        cost_estimate=SMALL,
        name="place",
    )(piece, *held)


def per_device(x_fwd, x_rev, gain, w_qkv):
    count = lax.axis_size("seq")
    index = lax.axis_index("seq")
    rows, width = x_fwd.shape
    scale = (width // HEADS) ** (-0.5) * LOG2E
    gain = gain.reshape(1, width)
    sibling = [(i, i ^ 1) for i in range(count)]
    beside = [(i, i - 1 if i % 2 == 0 else i + 1) for i in range(1, count - 1)]
    mirror = [(i, count - 1 - i) for i in range(count)]
    firsts = [sum(CHUNKS[:k]) for k in range(len(CHUNKS))]
    parts = HEADS // 2 // CHUNKS[0]

    def send(x, pairs):
        return lax.ppermute(x, "seq", pairs)

    flags = jnp.stack([index % 2, ((index > 0) & (index < count - 1)).astype(jnp.int32)])

    f_x = send(x_fwd, beside)
    f_y = send(x_fwd, sibling)
    s_y = send(x_rev, sibling)
    f_q, f_chip = project([x_fwd, f_y], gain, w_qkv, scale, False, True)
    s_q, s_chip = project([after(x_rev, f_q), s_y], gain, w_qkv, scale, True, True)
    s_x = send(after(x_rev, s_q), beside)

    a_moved = []
    f_x = after(f_x, s_q)
    f_rem = project([f_x], gain, w_qkv, scale, False, False, 0, parts)
    flags = after(flags, f_rem)
    for k in range(len(CHUNKS)):
        if k == 2:
            a_moved[0], s_x, flags = lax.optimization_barrier((a_moved[0], s_x, flags))
        a = attention(f_q, f_chip, f_chip, f_rem, flags, firsts[k], CHUNKS[k])
        flags = after(flags, a)
        if k == 0:
            f_rem = project([after(f_x, a)], gain, w_qkv, scale, False, False)
        a_moved.append(send(a, mirror))
    s_rem = project([after(s_x, a)], gain, w_qkv, scale, True, False)

    mine, moved, fwd, rev = [], [], None, None
    last = len(CHUNKS) - 1
    for k in range(last + 1):
        ahead = min(k + 1, last)
        a_moved[ahead], flags = lax.optimization_barrier((a_moved[ahead], flags))
        if k >= 2:
            rev = place(after(mine[k - 2], mine[k - 1]), firsts[k - 2], width, rev, True)
            fwd = place(after(moved[k - 2], rev), firsts[k - 2], width, fwd, False)
            flags = after(flags, fwd)
        y = attention(s_q, s_chip, s_chip, s_rem, flags, firsts[k], CHUNKS[k], a_moved[k])
        flags = after(flags, y)
        mine.append(y)
        moved.append(send(y, mirror))
    for k in (last - 1, last):
        rev = place(after(mine[k], mine[-1]), firsts[k], width, rev, True)
    for k in (last - 1, last):
        fwd = place(after(moved[k], rev), firsts[k], width, fwd, False)
    return fwd, rev


def solution(mesh):
    in_specs = (P(("dp", "seq"), None), P(("dp", "seq"), None), P(), P())
    out_specs = (P(("dp", "seq"), None), P(("dp", "seq"), None))
    return jax.shard_map(
        per_device, mesh=mesh, in_specs=in_specs, out_specs=out_specs, check_vma=False
    )
```

```python
import functools

import jax
import jax.numpy as jnp
from jax import lax
from jax.experimental import pallas as pl
from jax.experimental.pallas import tpu as pltpu
from jax.sharding import PartitionSpec as P

HEADS = 16
WINDOW = 512
LOG2E = 1.4426950408889634
NEG = -1e30
SMALL = pl.CostEstimate(flops=1, bytes_accessed=1, transcendentals=0)
VMEM_LIMIT = 64 * 1024 * 1024 - 256 * 1024
CHUNKS = (2, 3, 3)


def after(x, *others):
    return lax.optimization_barrier((x, *others))[0]


def exchange_matrix(n):
    r = lax.broadcasted_iota(jnp.int32, (n, n), 0)
    c = lax.broadcasted_iota(jnp.int32, (n, n), 1)
    return (r + c == n - 1).astype(jnp.bfloat16)


def rows_reversed(x, out_ref):
    half = x.shape[0] // 2
    ex = exchange_matrix(half)
    out_ref[:half] = jnp.dot(ex, x[half:], preferred_element_type=jnp.float32).astype(out_ref.dtype)
    out_ref[half:] = jnp.dot(ex, x[:half], preferred_element_type=jnp.float32).astype(out_ref.dtype)


def columns_reversed(x, out_ref):
    width = x.shape[1]
    size = min(256, width)
    ex = exchange_matrix(size)
    for n in range(width // size):
        t = jnp.dot(x[:, n * size : (n + 1) * size], ex, preferred_element_type=jnp.float32)
        out_ref[:, width - (n + 1) * size : width - n * size] = t.astype(out_ref.dtype)


def project_kernel(scale, mirrored, with_q, n, *refs):
    x_refs = refs[:n]
    gain_ref, w_ref = refs[n : n + 2]
    refs = refs[n + 2 :]
    if with_q:
        q_ref, kv_ref, hn_ref, turned_ref = refs
    else:
        kv_ref, hn_ref, turned_ref = refs
    j = pl.program_id(0)
    rows = x_refs[0].shape[0]

    @pl.when(j == 0)
    def _():
        for m in range(n):
            xf = x_refs[m][...].astype(jnp.float32)
            meansq = jnp.mean(xf * xf, axis=-1, keepdims=True)
            hn = xf * lax.rsqrt(meansq + 1e-6) * gain_ref[...].astype(jnp.float32)[None, :]
            hn_ref[m * rows : (m + 1) * rows] = hn.astype(jnp.bfloat16)

    def product(h):
        return jnp.dot(h, w_ref[...], preferred_element_type=jnp.float32)

    first = 1 if with_q else 0
    if with_q:

        @pl.when(j == 0)
        def _():
            if mirrored:
                rows_reversed(hn_ref[:rows], turned_ref)
                q_ref[...] = (product(turned_ref[...]) * scale).astype(jnp.bfloat16)
            else:
                q_ref[...] = (product(hn_ref[:rows]) * scale).astype(jnp.bfloat16)

    @pl.when(j == first)
    def _():
        kv_ref[...] = product(hn_ref[...]).astype(jnp.bfloat16)

    @pl.when(j == first + 1)
    def _():
        v = product(hn_ref[...]).astype(jnp.bfloat16)
        if mirrored:
            columns_reversed(v, kv_ref)
        else:
            kv_ref[...] = v


def project(xs, gain, w, scale, mirrored, with_q):
    rows, width = xs[0].shape
    n = len(xs)
    first = 1 if with_q else 0
    kv = jax.ShapeDtypeStruct((n * rows, 2 * width), jnp.bfloat16)
    kv_spec = pl.BlockSpec((n * rows, width), lambda j: (0, jnp.maximum(j - first, 0)))
    q = jax.ShapeDtypeStruct((rows, width), jnp.bfloat16)
    q_spec = pl.BlockSpec((rows, width), lambda j: (0, 0))
    return pl.pallas_call(
        functools.partial(project_kernel, scale, mirrored, with_q, n),
        out_shape=(q, kv) if with_q else kv,
        grid=(2 + first,),
        in_specs=[pl.BlockSpec((rows, width), lambda j: (0, 0))] * n
        + [
            pl.BlockSpec((width,), lambda j: (0,)),
            pl.BlockSpec((width, width), lambda j: (0, j + 1 - first)),
        ],
        out_specs=(q_spec, kv_spec) if with_q else kv_spec,
        scratch_shapes=[
            pltpu.VMEM((n * rows, width), jnp.bfloat16),
            pltpu.VMEM((rows, width), jnp.bfloat16),
        ],
        compiler_params=pltpu.CompilerParams(vmem_limit_bytes=VMEM_LIMIT),
        cost_estimate=SMALL,
        name="project",
    )(*xs, gain, w)


def attention_kernel(tile, mirrored, flags_ref, q_ref, ko_ref, ks_ref, kr_ref, vo_ref, vs_ref, vr_ref, *refs):
    if mirrored:
        near_ref, out_ref, kbuf, vbuf = refs
    else:
        out_ref, kbuf, vbuf = refs
    rows, width = q_ref.shape
    head = width // 2
    sibling_left = flags_ref[0] > 0
    has_remote = flags_ref[1] > 0
    at_s = pl.multiple_of(jnp.where(sibling_left, 0, 2 * rows), rows)
    at_r = pl.multiple_of(jnp.where(sibling_left, 2 * rows, 0), rows)
    ones = jnp.ones((rows, width), jnp.bfloat16)
    none = jnp.zeros((rows, width), jnp.bfloat16)
    kbuf[rows : 2 * rows] = ko_ref[...]
    vbuf[rows : 2 * rows, :width] = vo_ref[...]
    vbuf[rows : 2 * rows, width:] = ones
    kbuf[pl.ds(at_s, rows)] = ks_ref[...]
    vbuf[pl.ds(at_s, rows), :width] = vs_ref[...]
    vbuf[pl.ds(at_s, rows), width:] = ones
    kbuf[pl.ds(at_r, rows)] = jnp.where(has_remote, kr_ref[...], ko_ref[...])
    vbuf[pl.ds(at_r, rows), :width] = jnp.where(has_remote, vr_ref[...], none)
    vbuf[pl.ds(at_r, rows), width:] = jnp.where(has_remote, ones, none)

    span = tile + 2 * WINDOW
    r = lax.broadcasted_iota(jnp.int32, (tile, tile), 0)
    c = lax.broadcasted_iota(jnp.int32, (tile, tile), 1)
    if mirrored:
        r = tile - 1 - r
    low = c >= r
    high = c <= r
    lane = lax.broadcasted_iota(jnp.int32, (tile, width), 1)
    tiles = rows // tile
    for t in range(tiles):
        here = slice(t * tile, (t + 1) * tile)
        q = q_ref[here, :]
        first = (tiles - 1 - t if mirrored else t) * tile
        keys = kbuf[first : first + span, :]
        values = vbuf[first : first + span, :]
        outs = []
        for h in range(2):
            mine = (lane < head) if h == 0 else (lane >= head)
            qh = jnp.where(mine, q, jnp.zeros_like(q))
            s = lax.dot_general(
                qh, keys, (((1,), (1,)), ((), ())), preferred_element_type=jnp.float32
            )
            s_low = jnp.where(low, s[:, :tile], NEG)
            s_mid = s[:, tile : 2 * WINDOW]
            s_high = jnp.where(high, s[:, 2 * WINDOW :], NEG)
            s = jnp.concatenate([s_low, s_mid, s_high], axis=1)
            top = jnp.max(s, axis=-1, keepdims=True)
            p = jnp.exp2(s - top).astype(jnp.bfloat16)
            o = jnp.dot(p, values, preferred_element_type=jnp.float32)
            outs.append(o[:, :width] / o[:, width:])
        if mirrored:
            outs = outs[::-1]
        a = jnp.where(lane < head, outs[0], outs[1]).astype(jnp.bfloat16)
        if mirrored:
            a = (near_ref[here, :].astype(jnp.float32) + a.astype(jnp.float32)).astype(jnp.bfloat16)
        out_ref[here, :] = a


def attention(q, own, sibling, remote, flags, first, count, near=None):
    rows, width = q.shape
    pw = 2 * (width // HEADS)
    n = width // pw
    f = first
    mirrored = near is not None

    def key(g):
        return n - 1 - f - g if mirrored else f + g

    def keys(row):
        return pl.BlockSpec((rows, pw), lambda g: (row, key(g)))

    def values(row):
        return pl.BlockSpec((rows, pw), lambda g: (row, n + f + g))

    there = sibling.shape[0] // rows - 1
    out_spec = pl.BlockSpec((rows, pw), lambda g: (0, g))
    return pl.pallas_call(
        functools.partial(attention_kernel, min(256, rows), mirrored),
        out_shape=jax.ShapeDtypeStruct((rows, count * pw), jnp.bfloat16),
        grid=(count,),
        in_specs=[pl.BlockSpec(memory_space=pltpu.SMEM)]
        + [keys(0), keys(0), keys(there), keys(0), values(0), values(there), values(0)]
        + [out_spec] * mirrored,
        out_specs=out_spec,
        scratch_shapes=[
            pltpu.VMEM((rows + 2 * WINDOW, pw), jnp.bfloat16),
            pltpu.VMEM((rows + 2 * WINDOW, 2 * pw), jnp.bfloat16),
        ],
        compiler_params=pltpu.CompilerParams(vmem_limit_bytes=VMEM_LIMIT),
        cost_estimate=pl.CostEstimate(
            flops=4 * count * rows * (256 + 2 * WINDOW) * 2 * pw,
            bytes_accessed=4 * count * rows * pw,
            transcendentals=0,
        ),
        name="attention_mirrored" if mirrored else "attention",
    )(flags, q, own, sibling, remote, own, sibling, remote, *([near] if mirrored else []))


def turn_kernel(piece_ref, *refs):
    t = jnp.dot(piece_ref[...], exchange_matrix(piece_ref.shape[1]), preferred_element_type=jnp.float32)
    rows_reversed(t.astype(jnp.bfloat16), refs[-1])


def turn(piece, first, width, held):
    rows, columns = piece.shape
    pw = 2 * (width // HEADS)
    n = width // pw
    f = first
    held = [] if held is None else [held]
    return pl.pallas_call(
        turn_kernel,
        out_shape=jax.ShapeDtypeStruct((rows, width), jnp.bfloat16),
        grid=(columns // pw,),
        in_specs=[pl.BlockSpec((rows, pw), lambda g: (0, g))]
        + [pl.BlockSpec(memory_space=pl.ANY)] * len(held),
        out_specs=pl.BlockSpec((rows, pw), lambda g: (0, n - 1 - f - g)),
        input_output_aliases={1: 0} if held else {},
        compiler_params=pltpu.CompilerParams(vmem_limit_bytes=VMEM_LIMIT),
        cost_estimate=SMALL,
        name="turn",
    )(piece, *held)


def place_kernel(first, piece_ref, *refs):
    out_ref, sem = refs[-2:]
    copy = pltpu.make_async_copy(piece_ref, out_ref.at[:, pl.ds(first, piece_ref.shape[1])], sem)
    copy.start()
    copy.wait()


def place(piece, first, width, held):
    rows = piece.shape[0]
    held = [] if held is None else [held]
    anywhere = pl.BlockSpec(memory_space=pl.ANY)
    return pl.pallas_call(
        functools.partial(place_kernel, first * 2 * (width // HEADS)),
        out_shape=jax.ShapeDtypeStruct((rows, width), jnp.bfloat16),
        in_specs=[anywhere] * (1 + len(held)),
        out_specs=anywhere,
        scratch_shapes=[pltpu.SemaphoreType.DMA(())],
        input_output_aliases={1: 0} if held else {},
        compiler_params=pltpu.CompilerParams(vmem_limit_bytes=VMEM_LIMIT),
        cost_estimate=SMALL,
        name="place",
    )(piece, *held)


def per_device(x_fwd, x_rev, gain, w_qkv):
    count = lax.axis_size("seq")
    index = lax.axis_index("seq")
    rows, width = x_fwd.shape
    scale = (width // HEADS) ** (-0.5) * LOG2E
    sibling = [(i, i ^ 1) for i in range(count)]
    beside = [(i, i - 1 if i % 2 == 0 else i + 1) for i in range(1, count - 1)]
    mirror = [(i, count - 1 - i) for i in range(count)]
    firsts = [sum(CHUNKS[:k]) for k in range(len(CHUNKS))]

    def send(x, pairs):
        return lax.ppermute(x, "seq", pairs)

    flags = jnp.stack([index % 2, ((index > 0) & (index < count - 1)).astype(jnp.int32)])

    f_x = send(x_fwd, beside)
    f_y = send(x_fwd, sibling)
    s_y = send(x_rev, sibling)
    f_q, f_chip = project([after(x_fwd, flags), f_y], gain, w_qkv, scale, False, True)
    s_q, s_chip = project([after(x_rev, f_q), s_y], gain, w_qkv, scale, True, True)
    s_x = send(after(x_rev, s_q), beside)

    a_moved = []
    f_x = after(f_x, s_q)
    f_rem = project([f_x], gain, w_qkv, scale, False, False)
    flags = after(flags, f_rem)
    for k in range(len(CHUNKS)):
        if k == 2:
            a_moved[0], s_x, flags = lax.optimization_barrier((a_moved[0], s_x, flags))
        a = attention(f_q, f_chip, f_chip, f_rem, flags, firsts[k], CHUNKS[k])
        flags = after(flags, a)
        a_moved.append(send(a, mirror))
    s_rem = project([after(s_x, a)], gain, w_qkv, scale, True, False)

    mine, moved, fwd, rev = [], [], None, None
    last = len(CHUNKS) - 1
    for k in range(last + 1):
        ahead = min(k + 1, last)
        a_moved[ahead], flags = lax.optimization_barrier((a_moved[ahead], flags))
        if k >= 2:
            rev = turn(after(mine[k - 2], mine[k - 1]), firsts[k - 2], width, rev)
            fwd = place(after(moved[k - 2], rev), firsts[k - 2], width, fwd)
            flags = after(flags, fwd)
        y = attention(s_q, s_chip, s_chip, s_rem, flags, firsts[k], CHUNKS[k], a_moved[k])
        flags = after(flags, y)
        mine.append(y)
        moved.append(send(y, mirror))
    for k in (last - 1, last):
        rev = turn(after(mine[k], mine[-1]), firsts[k], width, rev)
    for k in (last - 1, last):
        fwd = place(after(moved[k], rev), firsts[k], width, fwd)
    return fwd, rev


def solution(mesh):
    in_specs = (P(("dp", "seq"), None), P(("dp", "seq"), None), P(), P())
    out_specs = (P(("dp", "seq"), None), P(("dp", "seq"), None))
    return jax.shard_map(
        per_device, mesh=mesh, in_specs=in_specs, out_specs=out_specs, check_vma=False
    )
```

```python
import functools

import jax
import jax.numpy as jnp
from jax import lax
from jax.experimental import pallas as pl
from jax.experimental.pallas import tpu as pltpu
from jax.sharding import PartitionSpec as P

HEADS = 16
WINDOW = 512
LOG2E = 1.4426950408889634
NEG = -1e30
SMALL = pl.CostEstimate(flops=1, bytes_accessed=1, transcendentals=0)
VMEM_LIMIT = 64 * 1024 * 1024 - 256 * 1024
CHUNKS = (2, 3, 3)


def after(x, *others):
    return lax.optimization_barrier((x, *others))[0]


def exchange_matrix(n):
    r = lax.broadcasted_iota(jnp.int32, (n, n), 0)
    c = lax.broadcasted_iota(jnp.int32, (n, n), 1)
    return (r + c == n - 1).astype(jnp.bfloat16)


def rows_reversed(x, out_ref):
    half = x.shape[0] // 2
    ex = exchange_matrix(half)
    out_ref[:half] = jnp.dot(ex, x[half:], preferred_element_type=jnp.float32).astype(out_ref.dtype)
    out_ref[half:] = jnp.dot(ex, x[:half], preferred_element_type=jnp.float32).astype(out_ref.dtype)


def columns_reversed(x, out_ref):
    width = x.shape[1]
    size = min(256, width)
    ex = exchange_matrix(size)
    for n in range(width // size):
        t = jnp.dot(x[:, n * size : (n + 1) * size], ex, preferred_element_type=jnp.float32)
        out_ref[:, width - (n + 1) * size : width - n * size] = t.astype(out_ref.dtype)


def project_kernel(scale, mirrored, with_q, n, *refs):
    x_refs = refs[:n]
    gain_ref, w_ref = refs[n : n + 2]
    refs = refs[n + 2 :]
    if with_q:
        q_ref, kv_ref, hn_ref, turned_ref = refs
    else:
        kv_ref, hn_ref, turned_ref = refs
    j = pl.program_id(0)
    rows = x_refs[0].shape[0]

    @pl.when(j == 0)
    def _():
        for m in range(n):
            xf = x_refs[m][...].astype(jnp.float32)
            meansq = jnp.mean(xf * xf, axis=-1, keepdims=True)
            hn = xf * lax.rsqrt(meansq + 1e-6) * gain_ref[...].astype(jnp.float32)[None, :]
            hn_ref[m * rows : (m + 1) * rows] = hn.astype(jnp.bfloat16)

    def product(h):
        return jnp.dot(h, w_ref[...], preferred_element_type=jnp.float32)

    first = 1 if with_q else 0
    if with_q:

        @pl.when(j == 0)
        def _():
            if mirrored:
                rows_reversed(hn_ref[:rows], turned_ref)
                q_ref[...] = (product(turned_ref[...]) * scale).astype(jnp.bfloat16)
            else:
                q_ref[...] = (product(hn_ref[:rows]) * scale).astype(jnp.bfloat16)

    @pl.when(j == first)
    def _():
        kv_ref[...] = product(hn_ref[...]).astype(jnp.bfloat16)

    @pl.when(j == first + 1)
    def _():
        v = product(hn_ref[...]).astype(jnp.bfloat16)
        if mirrored:
            columns_reversed(v, kv_ref)
        else:
            kv_ref[...] = v


def project(xs, gain, w, scale, mirrored, with_q):
    rows, width = xs[0].shape
    n = len(xs)
    first = 1 if with_q else 0
    kv = jax.ShapeDtypeStruct((n * rows, 2 * width), jnp.bfloat16)
    kv_spec = pl.BlockSpec((n * rows, width), lambda j: (0, jnp.maximum(j - first, 0)))
    q = jax.ShapeDtypeStruct((rows, width), jnp.bfloat16)
    q_spec = pl.BlockSpec((rows, width), lambda j: (0, 0))
    return pl.pallas_call(
        functools.partial(project_kernel, scale, mirrored, with_q, n),
        out_shape=(q, kv) if with_q else kv,
        grid=(2 + first,),
        in_specs=[pl.BlockSpec((rows, width), lambda j: (0, 0))] * n
        + [
            pl.BlockSpec((width,), lambda j: (0,)),
            pl.BlockSpec((width, width), lambda j: (0, j + 1 - first)),
        ],
        out_specs=(q_spec, kv_spec) if with_q else kv_spec,
        scratch_shapes=[
            pltpu.VMEM((n * rows, width), jnp.bfloat16),
            pltpu.VMEM((rows, width), jnp.bfloat16),
        ],
        compiler_params=pltpu.CompilerParams(vmem_limit_bytes=VMEM_LIMIT),
        cost_estimate=SMALL,
        name="project",
    )(*xs, gain, w)


def attention_kernel(tile, mirrored, flags_ref, q_ref, ko_ref, ks_ref, kr_ref, vo_ref, vs_ref, vr_ref, *refs):
    out_ref, kbuf, vbuf = refs
    rows, width = q_ref.shape
    head = width // 2
    sibling_left = flags_ref[0] > 0
    has_remote = flags_ref[1] > 0
    at_s = pl.multiple_of(jnp.where(sibling_left, 0, 2 * rows), rows)
    at_r = pl.multiple_of(jnp.where(sibling_left, 2 * rows, 0), rows)
    ones = jnp.ones((rows, width), jnp.bfloat16)
    none = jnp.zeros((rows, width), jnp.bfloat16)
    kbuf[rows : 2 * rows] = ko_ref[...]
    vbuf[rows : 2 * rows, :width] = vo_ref[...]
    vbuf[rows : 2 * rows, width:] = ones
    kbuf[pl.ds(at_s, rows)] = ks_ref[...]
    vbuf[pl.ds(at_s, rows), :width] = vs_ref[...]
    vbuf[pl.ds(at_s, rows), width:] = ones
    kbuf[pl.ds(at_r, rows)] = jnp.where(has_remote, kr_ref[...], ko_ref[...])
    vbuf[pl.ds(at_r, rows), :width] = jnp.where(has_remote, vr_ref[...], none)
    vbuf[pl.ds(at_r, rows), width:] = jnp.where(has_remote, ones, none)

    span = tile + 2 * WINDOW
    r = lax.broadcasted_iota(jnp.int32, (tile, tile), 0)
    c = lax.broadcasted_iota(jnp.int32, (tile, tile), 1)
    if mirrored:
        r = tile - 1 - r
    low = c >= r
    high = c <= r
    lane = lax.broadcasted_iota(jnp.int32, (tile, width), 1)
    tiles = rows // tile
    for t in range(tiles):
        here = slice(t * tile, (t + 1) * tile)
        q = q_ref[here, :]
        first = (tiles - 1 - t if mirrored else t) * tile
        keys = kbuf[first : first + span, :]
        values = vbuf[first : first + span, :]
        outs = []
        for h in range(2):
            mine = (lane < head) if h == 0 else (lane >= head)
            qh = jnp.where(mine, q, jnp.zeros_like(q))
            s = lax.dot_general(
                qh, keys, (((1,), (1,)), ((), ())), preferred_element_type=jnp.float32
            )
            s_low = jnp.where(low, s[:, :tile], NEG)
            s_mid = s[:, tile : 2 * WINDOW]
            s_high = jnp.where(high, s[:, 2 * WINDOW :], NEG)
            s = jnp.concatenate([s_low, s_mid, s_high], axis=1)
            top = jnp.max(s, axis=-1, keepdims=True)
            p = jnp.exp2(s - top).astype(jnp.bfloat16)
            o = jnp.dot(p, values, preferred_element_type=jnp.float32)
            outs.append(o[:, :width] / o[:, width:])
        if mirrored:
            outs = outs[::-1]
        a = jnp.where(lane < head, outs[0], outs[1]).astype(jnp.bfloat16)
        out_ref[here, :] = a


def attention(q, own, sibling, remote, flags, first, count, mirrored):
    rows, width = q.shape
    pw = 2 * (width // HEADS)
    n = width // pw
    f = first

    def key(g):
        return n - 1 - f - g if mirrored else f + g

    def keys(row):
        return pl.BlockSpec((rows, pw), lambda g: (row, key(g)))

    def values(row):
        return pl.BlockSpec((rows, pw), lambda g: (row, n + f + g))

    there = sibling.shape[0] // rows - 1
    out_spec = pl.BlockSpec((rows, pw), lambda g: (0, g))
    return pl.pallas_call(
        functools.partial(attention_kernel, min(256, rows), mirrored),
        out_shape=jax.ShapeDtypeStruct((rows, count * pw), jnp.bfloat16),
        grid=(count,),
        in_specs=[pl.BlockSpec(memory_space=pltpu.SMEM)]
        + [keys(0), keys(0), keys(there), keys(0), values(0), values(there), values(0)],
        out_specs=out_spec,
        scratch_shapes=[
            pltpu.VMEM((rows + 2 * WINDOW, pw), jnp.bfloat16),
            pltpu.VMEM((rows + 2 * WINDOW, 2 * pw), jnp.bfloat16),
        ],
        compiler_params=pltpu.CompilerParams(vmem_limit_bytes=VMEM_LIMIT),
        cost_estimate=pl.CostEstimate(
            flops=4 * count * rows * (256 + 2 * WINDOW) * 2 * pw // 1,
            bytes_accessed=count * rows * pw // 1,
            transcendentals=0,
        ),
        name="attention_mirrored" if mirrored else "attention",
    )(flags, q, own, sibling, remote, own, sibling, remote)


def added(a_ref, b_ref):
    return (a_ref[...].astype(jnp.float32) + b_ref[...].astype(jnp.float32)).astype(jnp.bfloat16)


def turn_kernel(a_ref, b_ref, *refs):
    t = jnp.dot(added(a_ref, b_ref), exchange_matrix(a_ref.shape[1]), preferred_element_type=jnp.float32)
    rows_reversed(t.astype(jnp.bfloat16), refs[-1])


def turn(a, b, first, width, held):
    rows, columns = a.shape
    pw = 2 * (width // HEADS)
    n = width // pw
    f = first
    held = [] if held is None else [held]
    block = pl.BlockSpec((rows, pw), lambda g: (0, g))
    return pl.pallas_call(
        turn_kernel,
        out_shape=jax.ShapeDtypeStruct((rows, width), jnp.bfloat16),
        grid=(columns // pw,),
        in_specs=[block, block] + [pl.BlockSpec(memory_space=pl.ANY)] * len(held),
        out_specs=pl.BlockSpec((rows, pw), lambda g: (0, n - 1 - f - g)),
        input_output_aliases={2: 0} if held else {},
        compiler_params=pltpu.CompilerParams(vmem_limit_bytes=VMEM_LIMIT),
        cost_estimate=SMALL,
        name="turn",
    )(a, b, *held)


def place_kernel(first, a_ref, b_ref, *refs):
    out_ref, sum_ref, sem = refs[-3:]
    sum_ref[...] = added(a_ref, b_ref)
    copy = pltpu.make_async_copy(sum_ref, out_ref.at[:, pl.ds(first, sum_ref.shape[1])], sem)
    copy.start()
    copy.wait()


def place(a, b, first, width, held):
    rows = a.shape[0]
    held = [] if held is None else [held]
    anywhere = pl.BlockSpec(memory_space=pl.ANY)
    return pl.pallas_call(
        functools.partial(place_kernel, first * 2 * (width // HEADS)),
        out_shape=jax.ShapeDtypeStruct((rows, width), jnp.bfloat16),
        in_specs=[pl.BlockSpec(memory_space=pltpu.VMEM)] * 2 + [anywhere] * len(held),
        out_specs=anywhere,
        scratch_shapes=[pltpu.VMEM(a.shape, jnp.bfloat16), pltpu.SemaphoreType.DMA(())],
        input_output_aliases={2: 0} if held else {},
        compiler_params=pltpu.CompilerParams(vmem_limit_bytes=VMEM_LIMIT),
        cost_estimate=SMALL,
        name="place",
    )(a, b, *held)


def per_device(x_fwd, x_rev, gain, w_qkv):
    count = lax.axis_size("seq")
    index = lax.axis_index("seq")
    rows, width = x_fwd.shape
    scale = (width // HEADS) ** (-0.5) * LOG2E
    sibling = [(i, i ^ 1) for i in range(count)]
    beside = [(i, i - 1 if i % 2 == 0 else i + 1) for i in range(1, count - 1)]
    mirror = [(i, count - 1 - i) for i in range(count)]
    firsts = [sum(CHUNKS[:k]) for k in range(len(CHUNKS))]

    def send(x, pairs):
        return lax.ppermute(x, "seq", pairs)

    flags = jnp.stack([index % 2, ((index > 0) & (index < count - 1)).astype(jnp.int32)])

    f_x = send(x_fwd, beside)
    f_y = send(x_fwd, sibling)
    s_y = send(x_rev, sibling)
    f_q, f_chip = project([after(x_fwd, flags), f_y], gain, w_qkv, scale, False, True)
    s_q, s_chip = project([after(x_rev, f_q), s_y], gain, w_qkv, scale, True, True)
    s_x = send(after(x_rev, s_q), beside)

    last = len(CHUNKS) - 1
    f_x = after(f_x, s_q)
    f_rem = project([f_x], gain, w_qkv, scale, False, False)
    flags = after(flags, f_rem)
    a_f, f_moved = [], []
    for k in range(last + 1):
        if k == last:
            f_moved[0], s_x, flags = lax.optimization_barrier((f_moved[0], s_x, flags))
        a_f.append(attention(f_q, f_chip, f_chip, f_rem, flags, firsts[k], CHUNKS[k], False))
        flags = after(flags, a_f[k])
        f_moved.append(send(a_f[k], mirror))
    s_rem = project([after(s_x, a_f[last])], gain, w_qkv, scale, True, False)
    flags = after(flags, s_rem)
    a_s, s_moved = [], []
    for k in range(last + 1):
        if 1 <= k <= last:
            f_moved[k], flags = lax.optimization_barrier((f_moved[k], flags))
        if 0 <= k - 2:
            s_moved[k - 2], flags = lax.optimization_barrier((s_moved[k - 2], flags))
        a_s.append(attention(s_q, s_chip, s_chip, s_rem, flags, firsts[k], CHUNKS[k], True))
        flags = after(flags, a_s[k])
        s_moved.append(send(a_s[k], mirror))
    fwd, rev = None, None
    for k in range(last + 1):
        rev = turn(after(a_s[k], a_s[last]), f_moved[k], firsts[k], width, rev)
    for k in range(last + 1):
        fwd = place(after(a_f[k], rev), s_moved[k], firsts[k], width, fwd)
    return fwd, rev


def solution(mesh):
    in_specs = (P(("dp", "seq"), None), P(("dp", "seq"), None), P(), P())
    out_specs = (P(("dp", "seq"), None), P(("dp", "seq"), None))
    return jax.shard_map(
        per_device, mesh=mesh, in_specs=in_specs, out_specs=out_specs, check_vma=False
    )
```

```python
import functools

import jax
import jax.numpy as jnp
from jax import lax
from jax.experimental import pallas as pl
from jax.experimental.pallas import tpu as pltpu
from jax.sharding import PartitionSpec as P

HEADS = 16
WINDOW = 512
LOG2E = 1.4426950408889634
NEG = -1e30
SMALL = pl.CostEstimate(flops=1, bytes_accessed=1, transcendentals=0)
VMEM_LIMIT = 64 * 1024 * 1024 - 256 * 1024
CHUNKS = (2, 3, 3)


def after(x, *others):
    return lax.optimization_barrier((x, *others))[0]


def exchange_matrix(n):
    r = lax.broadcasted_iota(jnp.int32, (n, n), 0)
    c = lax.broadcasted_iota(jnp.int32, (n, n), 1)
    return (r + c == n - 1).astype(jnp.bfloat16)


def rows_reversed(x, out_ref):
    half = x.shape[0] // 2
    ex = exchange_matrix(half)
    out_ref[:half] = jnp.dot(ex, x[half:], preferred_element_type=jnp.float32).astype(out_ref.dtype)
    out_ref[half:] = jnp.dot(ex, x[:half], preferred_element_type=jnp.float32).astype(out_ref.dtype)


def columns_reversed(x, out_ref):
    width = x.shape[1]
    size = min(256, width)
    ex = exchange_matrix(size)
    for n in range(width // size):
        t = jnp.dot(x[:, n * size : (n + 1) * size], ex, preferred_element_type=jnp.float32)
        out_ref[:, width - (n + 1) * size : width - n * size] = t.astype(out_ref.dtype)


def project_kernel(scale, mirrored, with_q, n, *refs):
    x_refs = refs[:n]
    gain_ref, w_ref = refs[n : n + 2]
    refs = refs[n + 2 :]
    if with_q:
        q_ref, kv_ref, hn_ref, turned_ref = refs
    else:
        kv_ref, hn_ref, turned_ref = refs
    j = pl.program_id(0)
    rows = x_refs[0].shape[0]

    @pl.when(j == 0)
    def _():
        for m in range(n):
            xf = x_refs[m][...].astype(jnp.float32)
            meansq = jnp.mean(xf * xf, axis=-1, keepdims=True)
            hn = xf * lax.rsqrt(meansq + 1e-6) * gain_ref[...].astype(jnp.float32)[None, :]
            hn_ref[m * rows : (m + 1) * rows] = hn.astype(jnp.bfloat16)

    def product(h):
        return jnp.dot(h, w_ref[...], preferred_element_type=jnp.float32)

    first = 1 if with_q else 0
    if with_q:

        @pl.when(j == 0)
        def _():
            if mirrored:
                rows_reversed(hn_ref[:rows], turned_ref)
                q_ref[...] = (product(turned_ref[...]) * scale).astype(jnp.bfloat16)
            else:
                q_ref[...] = (product(hn_ref[:rows]) * scale).astype(jnp.bfloat16)

    @pl.when(j == first)
    def _():
        kv_ref[...] = product(hn_ref[...]).astype(jnp.bfloat16)

    @pl.when(j == first + 1)
    def _():
        v = product(hn_ref[...]).astype(jnp.bfloat16)
        if mirrored:
            columns_reversed(v, kv_ref)
        else:
            kv_ref[...] = v


def project(xs, gain, w, scale, mirrored, with_q):
    rows, width = xs[0].shape
    n = len(xs)
    first = 1 if with_q else 0
    kv = jax.ShapeDtypeStruct((n * rows, 2 * width), jnp.bfloat16)
    kv_spec = pl.BlockSpec((n * rows, width), lambda j: (0, jnp.maximum(j - first, 0)))
    q = jax.ShapeDtypeStruct((rows, width), jnp.bfloat16)
    q_spec = pl.BlockSpec((rows, width), lambda j: (0, 0))
    return pl.pallas_call(
        functools.partial(project_kernel, scale, mirrored, with_q, n),
        out_shape=(q, kv) if with_q else kv,
        grid=(2 + first,),
        in_specs=[pl.BlockSpec((rows, width), lambda j: (0, 0))] * n
        + [
            pl.BlockSpec((width,), lambda j: (0,)),
            pl.BlockSpec((width, width), lambda j: (0, j + 1 - first)),
        ],
        out_specs=(q_spec, kv_spec) if with_q else kv_spec,
        scratch_shapes=[
            pltpu.VMEM((n * rows, width), jnp.bfloat16),
            pltpu.VMEM((rows, width), jnp.bfloat16),
        ],
        compiler_params=pltpu.CompilerParams(vmem_limit_bytes=VMEM_LIMIT),
        cost_estimate=SMALL,
        name="project",
    )(*xs, gain, w)


def attention_kernel(tile, mirrored, flags_ref, q_ref, ko_ref, ks_ref, kr_ref, vo_ref, vs_ref, vr_ref, *refs):
    out_ref, kbuf, vbuf = refs
    rows, width = q_ref.shape
    head = width // 2
    sibling_left = flags_ref[0] > 0
    has_remote = flags_ref[1] > 0
    at_s = pl.multiple_of(jnp.where(sibling_left, 0, 2 * rows), rows)
    at_r = pl.multiple_of(jnp.where(sibling_left, 2 * rows, 0), rows)
    ones = jnp.ones((rows, width), jnp.bfloat16)
    none = jnp.zeros((rows, width), jnp.bfloat16)
    kbuf[rows : 2 * rows] = ko_ref[...]
    vbuf[rows : 2 * rows, :width] = vo_ref[...]
    vbuf[rows : 2 * rows, width:] = ones
    kbuf[pl.ds(at_s, rows)] = ks_ref[...]
    vbuf[pl.ds(at_s, rows), :width] = vs_ref[...]
    vbuf[pl.ds(at_s, rows), width:] = ones
    kbuf[pl.ds(at_r, rows)] = jnp.where(has_remote, kr_ref[...], ko_ref[...])
    vbuf[pl.ds(at_r, rows), :width] = jnp.where(has_remote, vr_ref[...], none)
    vbuf[pl.ds(at_r, rows), width:] = jnp.where(has_remote, ones, none)

    span = tile + 2 * WINDOW
    r = lax.broadcasted_iota(jnp.int32, (tile, tile), 0)
    c = lax.broadcasted_iota(jnp.int32, (tile, tile), 1)
    if mirrored:
        r = tile - 1 - r
    low = c >= r
    high = c <= r
    lane = lax.broadcasted_iota(jnp.int32, (tile, width), 1)
    tiles = rows // tile
    for t in range(tiles):
        here = slice(t * tile, (t + 1) * tile)
        q = q_ref[here, :]
        first = (tiles - 1 - t if mirrored else t) * tile
        keys = kbuf[first : first + span, :]
        values = vbuf[first : first + span, :]
        outs = []
        for h in range(2):
            mine = (lane < head) if h == 0 else (lane >= head)
            qh = jnp.where(mine, q, jnp.zeros_like(q))
            s = lax.dot_general(
                qh, keys, (((1,), (1,)), ((), ())), preferred_element_type=jnp.float32
            )
            s_low = jnp.where(low, s[:, :tile], NEG)
            s_mid = s[:, tile : 2 * WINDOW]
            s_high = jnp.where(high, s[:, 2 * WINDOW :], NEG)
            s = jnp.concatenate([s_low, s_mid, s_high], axis=1)
            top = jnp.max(s, axis=-1, keepdims=True)
            p = jnp.exp2(s - top).astype(jnp.bfloat16)
            o = jnp.dot(p, values, preferred_element_type=jnp.float32)
            outs.append(o[:, :width] / o[:, width:])
        if mirrored:
            outs = outs[::-1]
        a = jnp.where(lane < head, outs[0], outs[1]).astype(jnp.bfloat16)
        out_ref[here, :] = a


def attention(q, own, sibling, remote, flags, first, count, mirrored):
    rows, width = q.shape
    pw = 2 * (width // HEADS)
    n = width // pw
    f = first

    def key(g):
        return n - 1 - f - g if mirrored else f + g

    def keys(row):
        return pl.BlockSpec((rows, pw), lambda g: (row, key(g)))

    def values(row):
        return pl.BlockSpec((rows, pw), lambda g: (row, n + f + g))

    there = sibling.shape[0] // rows - 1
    out_spec = pl.BlockSpec((rows, pw), lambda g: (0, g))
    return pl.pallas_call(
        functools.partial(attention_kernel, min(256, rows), mirrored),
        out_shape=jax.ShapeDtypeStruct((rows, count * pw), jnp.bfloat16),
        grid=(count,),
        in_specs=[pl.BlockSpec(memory_space=pltpu.SMEM)]
        + [keys(0), keys(0), keys(there), keys(0), values(0), values(there), values(0)],
        out_specs=out_spec,
        scratch_shapes=[
            pltpu.VMEM((rows + 2 * WINDOW, pw), jnp.bfloat16),
            pltpu.VMEM((rows + 2 * WINDOW, 2 * pw), jnp.bfloat16),
        ],
        compiler_params=pltpu.CompilerParams(vmem_limit_bytes=VMEM_LIMIT),
        cost_estimate=pl.CostEstimate(
            flops=4 * count * rows * (256 + 2 * WINDOW) * 2 * pw // 1,
            bytes_accessed=count * rows * pw // 1,
            transcendentals=0,
        ),
        name="attention_mirrored" if mirrored else "attention",
    )(flags, q, own, sibling, remote, own, sibling, remote)


def added(a_ref, b_ref):
    return (a_ref[...].astype(jnp.float32) + b_ref[...].astype(jnp.float32)).astype(jnp.bfloat16)


def turn_kernel(a_ref, b_ref, *refs):
    t = jnp.dot(added(a_ref, b_ref), exchange_matrix(a_ref.shape[1]), preferred_element_type=jnp.float32)
    rows_reversed(t.astype(jnp.bfloat16), refs[-1])


def turn(a, b, first, width, held):
    rows, columns = a.shape
    pw = 2 * (width // HEADS)
    n = width // pw
    f = first
    held = [] if held is None else [held]
    block = pl.BlockSpec((rows, pw), lambda g: (0, g))
    return pl.pallas_call(
        turn_kernel,
        out_shape=jax.ShapeDtypeStruct((rows, width), jnp.bfloat16),
        grid=(columns // pw,),
        in_specs=[block, block] + [pl.BlockSpec(memory_space=pl.ANY)] * len(held),
        out_specs=pl.BlockSpec((rows, pw), lambda g: (0, n - 1 - f - g)),
        input_output_aliases={2: 0} if held else {},
        compiler_params=pltpu.CompilerParams(vmem_limit_bytes=VMEM_LIMIT),
        cost_estimate=SMALL,
        name="turn",
    )(a, b, *held)


def place_kernel(first, a_ref, b_ref, *refs):
    out_ref, sum_ref, sem = refs[-3:]
    sum_ref[...] = added(a_ref, b_ref)
    copy = pltpu.make_async_copy(sum_ref, out_ref.at[:, pl.ds(first, sum_ref.shape[1])], sem)
    copy.start()
    copy.wait()


def place(a, b, first, width, held):
    rows = a.shape[0]
    held = [] if held is None else [held]
    anywhere = pl.BlockSpec(memory_space=pl.ANY)
    return pl.pallas_call(
        functools.partial(place_kernel, first * 2 * (width // HEADS)),
        out_shape=jax.ShapeDtypeStruct((rows, width), jnp.bfloat16),
        in_specs=[pl.BlockSpec(memory_space=pltpu.VMEM)] * 2 + [anywhere] * len(held),
        out_specs=anywhere,
        scratch_shapes=[pltpu.VMEM(a.shape, jnp.bfloat16), pltpu.SemaphoreType.DMA(())],
        input_output_aliases={2: 0} if held else {},
        compiler_params=pltpu.CompilerParams(vmem_limit_bytes=VMEM_LIMIT),
        cost_estimate=SMALL,
        name="place",
    )(a, b, *held)


def per_device(x_fwd, x_rev, gain, w_qkv):
    count = lax.axis_size("seq")
    index = lax.axis_index("seq")
    rows, width = x_fwd.shape
    scale = (width // HEADS) ** (-0.5) * LOG2E
    sibling = [(i, i ^ 1) for i in range(count)]
    beside = [(i, i - 1 if i % 2 == 0 else i + 1) for i in range(1, count - 1)]
    mirror = [(i, count - 1 - i) for i in range(count)]
    firsts = [sum(CHUNKS[:k]) for k in range(len(CHUNKS))]

    def send(x, pairs):
        return lax.ppermute(x, "seq", pairs)

    flags = jnp.stack([index % 2, ((index > 0) & (index < count - 1)).astype(jnp.int32)])

    f_x = send(x_fwd, beside)
    f_y = send(x_fwd, sibling)
    s_y = send(x_rev, sibling)
    f_q, f_chip = project([after(x_fwd, flags), f_y], gain, w_qkv, scale, False, True)
    s_q, s_chip = project([after(x_rev, f_q), s_y], gain, w_qkv, scale, True, True)
    s_x = send(after(x_rev, s_q), beside)

    last = len(CHUNKS) - 1
    f_x = after(f_x, s_q)
    f_rem = project([f_x], gain, w_qkv, scale, False, False)
    flags = after(flags, f_rem)
    a_f, f_moved = [], []
    for k in range(last + 1):
        if k == last:
            s_x, flags = lax.optimization_barrier((s_x, flags))
        a_f.append(attention(f_q, f_chip, f_chip, f_rem, flags, firsts[k], CHUNKS[k], False))
        flags = after(flags, a_f[k])
        f_moved.append(send(a_f[k], mirror))
    s_rem = project([after(s_x, a_f[last])], gain, w_qkv, scale, True, False)
    flags = after(flags, s_rem)
    f_moved[0], flags = lax.optimization_barrier((f_moved[0], flags))
    a_s, s_moved, fwd, rev = [], [], None, None
    for k in range(last + 1):
        if 1 <= k <= last:
            f_moved[k], flags = lax.optimization_barrier((f_moved[k], flags))
        if k == last:
            for m in range(last):
                rev = turn(after(a_s[m], a_s[last - 1]), f_moved[m], firsts[m], width, rev)
            s_moved[0], flags = lax.optimization_barrier((s_moved[0], flags, rev))[:2]
        a_s.append(attention(s_q, s_chip, s_chip, s_rem, flags, firsts[k], CHUNKS[k], True))
        flags = after(flags, a_s[k])
        s_moved.append(send(a_s[k], mirror))
    rev = turn(a_s[last], f_moved[last], firsts[last], width, rev)
    for k in range(last + 1):
        fwd = place(after(a_f[k], rev), s_moved[k], firsts[k], width, fwd)
    return fwd, rev


def solution(mesh):
    in_specs = (P(("dp", "seq"), None), P(("dp", "seq"), None), P(), P())
    out_specs = (P(("dp", "seq"), None), P(("dp", "seq"), None))
    return jax.shard_map(
        per_device, mesh=mesh, in_specs=in_specs, out_specs=out_specs, check_vma=False
    )
```

```python
import functools

import jax
import jax.numpy as jnp
from jax import lax
from jax.experimental import pallas as pl
from jax.experimental.pallas import tpu as pltpu
from jax.sharding import PartitionSpec as P

HEADS = 16
WINDOW = 512
LOG2E = 1.4426950408889634
NEG = -1e30
SMALL = pl.CostEstimate(flops=1, bytes_accessed=1, transcendentals=0)
VMEM_LIMIT = 64 * 1024 * 1024 - 256 * 1024
CHUNKS = (3, 3, 2)


def after(x, *others):
    return lax.optimization_barrier((x, *others))[0]


def exchange_matrix(n):
    r = lax.broadcasted_iota(jnp.int32, (n, n), 0)
    c = lax.broadcasted_iota(jnp.int32, (n, n), 1)
    return (r + c == n - 1).astype(jnp.bfloat16)


def rows_reversed(x, out_ref):
    half = x.shape[0] // 2
    ex = exchange_matrix(half)
    out_ref[:half] = jnp.dot(ex, x[half:], preferred_element_type=jnp.float32).astype(out_ref.dtype)
    out_ref[half:] = jnp.dot(ex, x[:half], preferred_element_type=jnp.float32).astype(out_ref.dtype)


def columns_reversed(x, out_ref):
    width = x.shape[1]
    size = min(256, width)
    ex = exchange_matrix(size)
    for n in range(width // size):
        t = jnp.dot(x[:, n * size : (n + 1) * size], ex, preferred_element_type=jnp.float32)
        out_ref[:, width - (n + 1) * size : width - n * size] = t.astype(out_ref.dtype)


def project_kernel(scale, mirrored, with_q, n, *refs):
    x_refs = refs[:n]
    gain_ref, w_ref = refs[n : n + 2]
    refs = refs[n + 2 :]
    if with_q:
        q_ref, kv_ref, hn_ref, turned_ref = refs
    else:
        kv_ref, hn_ref, turned_ref = refs
    j = pl.program_id(0)
    rows = x_refs[0].shape[0]

    @pl.when(j == 0)
    def _():
        for m in range(n):
            xf = x_refs[m][...].astype(jnp.float32)
            meansq = jnp.mean(xf * xf, axis=-1, keepdims=True)
            hn = xf * lax.rsqrt(meansq + 1e-6) * gain_ref[...].astype(jnp.float32)[None, :]
            hn_ref[m * rows : (m + 1) * rows] = hn.astype(jnp.bfloat16)

    def product(h):
        return jnp.dot(h, w_ref[...], preferred_element_type=jnp.float32)

    first = 1 if with_q else 0
    if with_q:

        @pl.when(j == 0)
        def _():
            if mirrored:
                rows_reversed(hn_ref[:rows], turned_ref)
                q_ref[...] = (product(turned_ref[...]) * scale).astype(jnp.bfloat16)
            else:
                q_ref[...] = (product(hn_ref[:rows]) * scale).astype(jnp.bfloat16)

    @pl.when(j == first)
    def _():
        kv_ref[...] = product(hn_ref[...]).astype(jnp.bfloat16)

    @pl.when(j == first + 1)
    def _():
        v = product(hn_ref[...]).astype(jnp.bfloat16)
        if mirrored:
            columns_reversed(v, kv_ref)
        else:
            kv_ref[...] = v


def project(xs, gain, w, scale, mirrored, with_q):
    rows, width = xs[0].shape
    n = len(xs)
    first = 1 if with_q else 0
    kv = jax.ShapeDtypeStruct((n * rows, 2 * width), jnp.bfloat16)
    kv_spec = pl.BlockSpec((n * rows, width), lambda j: (0, jnp.maximum(j - first, 0)))
    q = jax.ShapeDtypeStruct((rows, width), jnp.bfloat16)
    q_spec = pl.BlockSpec((rows, width), lambda j: (0, 0))
    return pl.pallas_call(
        functools.partial(project_kernel, scale, mirrored, with_q, n),
        out_shape=(q, kv) if with_q else kv,
        grid=(2 + first,),
        in_specs=[pl.BlockSpec((rows, width), lambda j: (0, 0))] * n
        + [
            pl.BlockSpec((width,), lambda j: (0,)),
            pl.BlockSpec((width, width), lambda j: (0, j + 1 - first)),
        ],
        out_specs=(q_spec, kv_spec) if with_q else kv_spec,
        scratch_shapes=[
            pltpu.VMEM((n * rows, width), jnp.bfloat16),
            pltpu.VMEM((rows, width), jnp.bfloat16),
        ],
        compiler_params=pltpu.CompilerParams(vmem_limit_bytes=VMEM_LIMIT),
        cost_estimate=SMALL,
        name="project",
    )(*xs, gain, w)


def attention_kernel(tile, mirrored, flags_ref, q_ref, ko_ref, ks_ref, kr_ref, vo_ref, vs_ref, vr_ref, *refs):
    out_ref, kbuf, vbuf = refs
    rows, width = q_ref.shape
    head = width // 2
    sibling_left = flags_ref[0] > 0
    has_remote = flags_ref[1] > 0
    at_s = pl.multiple_of(jnp.where(sibling_left, 0, 2 * rows), rows)
    at_r = pl.multiple_of(jnp.where(sibling_left, 2 * rows, 0), rows)
    ones = jnp.ones((rows, width), jnp.bfloat16)
    none = jnp.zeros((rows, width), jnp.bfloat16)
    kbuf[rows : 2 * rows] = ko_ref[...]
    vbuf[rows : 2 * rows, :width] = vo_ref[...]
    vbuf[rows : 2 * rows, width:] = ones
    kbuf[pl.ds(at_s, rows)] = ks_ref[...]
    vbuf[pl.ds(at_s, rows), :width] = vs_ref[...]
    vbuf[pl.ds(at_s, rows), width:] = ones
    kbuf[pl.ds(at_r, rows)] = jnp.where(has_remote, kr_ref[...], ko_ref[...])
    vbuf[pl.ds(at_r, rows), :width] = jnp.where(has_remote, vr_ref[...], none)
    vbuf[pl.ds(at_r, rows), width:] = jnp.where(has_remote, ones, none)

    span = tile + 2 * WINDOW
    r = lax.broadcasted_iota(jnp.int32, (tile, tile), 0)
    c = lax.broadcasted_iota(jnp.int32, (tile, tile), 1)
    if mirrored:
        r = tile - 1 - r
    low = c >= r
    high = c <= r
    lane = lax.broadcasted_iota(jnp.int32, (tile, width), 1)
    tiles = rows // tile
    for t in range(tiles):
        here = slice(t * tile, (t + 1) * tile)
        q = q_ref[here, :]
        first = (tiles - 1 - t if mirrored else t) * tile
        keys = kbuf[first : first + span, :]
        values = vbuf[first : first + span, :]
        outs = []
        for h in range(2):
            mine = (lane < head) if h == 0 else (lane >= head)
            qh = jnp.where(mine, q, jnp.zeros_like(q))
            s = lax.dot_general(
                qh, keys, (((1,), (1,)), ((), ())), preferred_element_type=jnp.float32
            )
            s_low = jnp.where(low, s[:, :tile], NEG)
            s_mid = s[:, tile : 2 * WINDOW]
            s_high = jnp.where(high, s[:, 2 * WINDOW :], NEG)
            s = jnp.concatenate([s_low, s_mid, s_high], axis=1)
            top = jnp.max(s, axis=-1, keepdims=True)
            p = jnp.exp2(s - top).astype(jnp.bfloat16)
            o = jnp.dot(p, values, preferred_element_type=jnp.float32)
            outs.append(o[:, :width] / o[:, width:])
        if mirrored:
            outs = outs[::-1]
        a = jnp.where(lane < head, outs[0], outs[1]).astype(jnp.bfloat16)
        out_ref[here, :] = a


def attention(q, own, sibling, remote, flags, first, count, mirrored):
    rows, width = q.shape
    pw = 2 * (width // HEADS)
    n = width // pw
    f = first

    def key(g):
        return n - 1 - f - g if mirrored else f + g

    def keys(row):
        return pl.BlockSpec((rows, pw), lambda g: (row, key(g)))

    def values(row):
        return pl.BlockSpec((rows, pw), lambda g: (row, n + f + g))

    there = sibling.shape[0] // rows - 1
    out_spec = pl.BlockSpec((rows, pw), lambda g: (0, g))
    return pl.pallas_call(
        functools.partial(attention_kernel, min(256, rows), mirrored),
        out_shape=jax.ShapeDtypeStruct((rows, count * pw), jnp.bfloat16),
        grid=(count,),
        in_specs=[pl.BlockSpec(memory_space=pltpu.SMEM)]
        + [keys(0), keys(0), keys(there), keys(0), values(0), values(there), values(0)],
        out_specs=out_spec,
        scratch_shapes=[
            pltpu.VMEM((rows + 2 * WINDOW, pw), jnp.bfloat16),
            pltpu.VMEM((rows + 2 * WINDOW, 2 * pw), jnp.bfloat16),
        ],
        compiler_params=pltpu.CompilerParams(vmem_limit_bytes=VMEM_LIMIT),
        cost_estimate=pl.CostEstimate(
            flops=4 * count * rows * (256 + 2 * WINDOW) * 2 * pw // 1,
            bytes_accessed=count * rows * pw // 1,
            transcendentals=0,
        ),
        name="attention_mirrored" if mirrored else "attention",
    )(flags, q, own, sibling, remote, own, sibling, remote)


def added(a_ref, b_ref):
    return (a_ref[...].astype(jnp.float32) + b_ref[...].astype(jnp.float32)).astype(jnp.bfloat16)


def turn_kernel(a_ref, b_ref, *refs):
    t = jnp.dot(added(a_ref, b_ref), exchange_matrix(a_ref.shape[1]), preferred_element_type=jnp.float32)
    rows_reversed(t.astype(jnp.bfloat16), refs[-1])


def turn(a, b, first, width, held):
    rows, columns = a.shape
    pw = 2 * (width // HEADS)
    n = width // pw
    f = first
    held = [] if held is None else [held]
    block = pl.BlockSpec((rows, pw), lambda g: (0, g))
    return pl.pallas_call(
        turn_kernel,
        out_shape=jax.ShapeDtypeStruct((rows, width), jnp.bfloat16),
        grid=(columns // pw,),
        in_specs=[block, block] + [pl.BlockSpec(memory_space=pl.ANY)] * len(held),
        out_specs=pl.BlockSpec((rows, pw), lambda g: (0, n - 1 - f - g)),
        input_output_aliases={2: 0} if held else {},
        compiler_params=pltpu.CompilerParams(vmem_limit_bytes=VMEM_LIMIT),
        cost_estimate=SMALL,
        name="turn",
    )(a, b, *held)


def place_kernel(first, a_ref, b_ref, *refs):
    out_ref, sum_ref, sem = refs[-3:]
    sum_ref[...] = added(a_ref, b_ref)
    copy = pltpu.make_async_copy(sum_ref, out_ref.at[:, pl.ds(first, sum_ref.shape[1])], sem)
    copy.start()
    copy.wait()


def place(a, b, first, width, held):
    rows = a.shape[0]
    held = [] if held is None else [held]
    anywhere = pl.BlockSpec(memory_space=pl.ANY)
    return pl.pallas_call(
        functools.partial(place_kernel, first * 2 * (width // HEADS)),
        out_shape=jax.ShapeDtypeStruct((rows, width), jnp.bfloat16),
        in_specs=[pl.BlockSpec(memory_space=pltpu.VMEM)] * 2 + [anywhere] * len(held),
        out_specs=anywhere,
        scratch_shapes=[pltpu.VMEM(a.shape, jnp.bfloat16), pltpu.SemaphoreType.DMA(())],
        input_output_aliases={2: 0} if held else {},
        compiler_params=pltpu.CompilerParams(vmem_limit_bytes=VMEM_LIMIT),
        cost_estimate=SMALL,
        name="place",
    )(a, b, *held)


def per_device(x_fwd, x_rev, gain, w_qkv):
    count = lax.axis_size("seq")
    index = lax.axis_index("seq")
    rows, width = x_fwd.shape
    scale = (width // HEADS) ** (-0.5) * LOG2E
    sibling = [(i, i ^ 1) for i in range(count)]
    beside = [(i, i - 1 if i % 2 == 0 else i + 1) for i in range(1, count - 1)]
    mirror = [(i, count - 1 - i) for i in range(count)]
    firsts = [sum(CHUNKS[:k]) for k in range(len(CHUNKS))]

    def send(x, pairs):
        return lax.ppermute(x, "seq", pairs)

    flags = jnp.stack([index % 2, ((index > 0) & (index < count - 1)).astype(jnp.int32)])

    f_x = send(x_fwd, beside)
    f_y = send(x_fwd, sibling)
    s_y = send(x_rev, sibling)
    f_q, f_chip = project([after(x_fwd, flags), f_y], gain, w_qkv, scale, False, True)
    s_q, s_chip = project([after(x_rev, f_q), s_y], gain, w_qkv, scale, True, True)
    s_x = send(after(x_rev, s_q), beside)

    last = len(CHUNKS) - 1
    f_x = after(f_x, s_q)
    f_rem = project([f_x], gain, w_qkv, scale, False, False)
    flags = after(flags, f_rem)
    a_f, f_moved = [], []
    for k in range(last + 1):
        if k == last:
            s_x, flags = lax.optimization_barrier((s_x, flags))
        a_f.append(attention(f_q, f_chip, f_chip, f_rem, flags, firsts[k], CHUNKS[k], False))
        flags = after(flags, a_f[k])
        f_moved.append(send(a_f[k], mirror))
    s_rem = project([after(s_x, a_f[last])], gain, w_qkv, scale, True, False)
    flags = after(flags, s_rem)
    f_moved[0], flags = lax.optimization_barrier((f_moved[0], flags))
    a_s, s_moved, fwd, rev = [], [], None, None
    for k in range(last + 1):
        if 1 <= k <= last:
            f_moved[k], flags = lax.optimization_barrier((f_moved[k], flags))
        if k == last:
            for m in range(last):
                rev = turn(after(a_s[m], a_s[last - 1]), f_moved[m], firsts[m], width, rev)
            s_moved[0], flags = lax.optimization_barrier((s_moved[0], flags, rev))[:2]
        a_s.append(attention(s_q, s_chip, s_chip, s_rem, flags, firsts[k], CHUNKS[k], True))
        flags = after(flags, a_s[k])
        s_moved.append(send(a_s[k], mirror))
    rev = turn(a_s[last], f_moved[last], firsts[last], width, rev)
    for k in range(last + 1):
        fwd = place(after(a_f[k], rev), s_moved[k], firsts[k], width, fwd)
    return fwd, rev


def solution(mesh):
    in_specs = (P(("dp", "seq"), None), P(("dp", "seq"), None), P(), P())
    out_specs = (P(("dp", "seq"), None), P(("dp", "seq"), None))
    return jax.shard_map(
        per_device, mesh=mesh, in_specs=in_specs, out_specs=out_specs, check_vma=False
    )
```
